256 devices in a mesh: ctx: 8 (over x_hi, y), db: 32 (over z, x_lo, core).
Axes of the slice: x: 4 (x_hi: 2, x_lo: 2; x = x_hi * 2 + x_lo), y: 4, z: 8, core: 2. Of those that a mesh axis runs over, the one named last changes fastest.
Arguments:
- q_self: bfloat16 [8192, 4096], P('ctx', 'db'), may hold values from -144 to 144
- k_self: bfloat16 [8192, 4096], P('ctx', 'db'), may hold values from -6 to 6
- v_self: bfloat16 [8192, 4096], P('ctx', 'db'), may hold values from -8 to 8
- db_states: bfloat16 [512, 128, 896], P('db'), may hold values from -16 to 16
- nb_shard: int32 [128, 2], P('ctx'), may hold values from 0 to 31, all different within a row; in each aligned block of 16 rows (0 to 15, 16 to 31, ...) at most 2 rows name the same one
- nb_row: int32 [128, 2], P('ctx'), may hold values from 0 to 15
- wk_x: bfloat16 [896, 4096], P(None, 'db'), may hold values from -2 to 2
- wv_x: bfloat16 [896, 4096], P(None, 'db'), may hold values from -0.1875 to 0.1875
- wq_x: bfloat16 [4096, 4096], P(None, 'db'), may hold values from -2 to 2
Outputs:
- self_out: bfloat16 [8192, 4096], P('ctx', 'db')
- cross_out: bfloat16 [8192, 4096], P('ctx', 'db')
The draws below stay inside these ranges and needn't reach their ends.
Inputs may be any that keep to these rules, and one draw needn't show every extreme that they name: `nb_shard`: among the groups of one sequence block (16 consecutive groups) no shard is named more than 2 times, a bound that some block reaches; the 2 neighbours of a group lie on different shards.
All inputs are finite; a program needn't handle non-finite values.
Results may differ from the reference program's by a relative error of at most 0.013.
The reference program's roundings to bfloat16 on the way count: a program that leaves them out, or rounds other values in their place, can miss the bound.
Values may be sent and summed in bfloat16 or wider, within the bound.
No kernel may reach another device: no remote copies, remote signals or barrier semaphores. Data moves between devices by JAX's collectives and lax.ppermute only.
A program may use at most 128 MiB of HBM per device.

```python
import math
import jax
import jax.numpy as jnp
import numpy as np
from jax import lax

HD = 128
E = 896
GROUP = 64
NT = 128
KNB = 2
R_DEV = 16
HEADS = 32
D = 4096
SEQ = 8192
GROUP_DEV = 16
GROUPS = 128
DB_ROWS = 512
MOST = 2
N_DB = 32


def paired_draw(key):
    keys_part = jnp.clip(jax.random.normal(jax.random.fold_in(key, 11), (SEQ, D), jnp.float32), -6.0, 6.0)
    queries = jnp.clip(2.5 * jax.random.normal(jax.random.fold_in(key, 12), (SEQ, D), jnp.float32), -15.0, 15.0)
    return (queries, keys_part)


def draw_q_self(key, part):
    return paired_draw(key)[0].astype(jnp.bfloat16)


def draw_k_self(key, part):
    return paired_draw(key)[1].astype(jnp.bfloat16)


def draw_v_self(key, part):
    values = jnp.clip(jax.random.normal(jax.random.fold_in(key, 31), (SEQ, D), jnp.float32), -6.0, 6.0)
    return values.astype(jnp.bfloat16)


def draw_wq_x(key, part):
    matrix = jnp.clip(jax.random.normal(jax.random.fold_in(key, 32), (D, D), jnp.float32), -6.0, 6.0) * (6.0 / math.sqrt(D))
    return matrix.astype(jnp.bfloat16)


def draw_wk_x(key, part):
    matrix = jnp.clip(jax.random.normal(jax.random.fold_in(key, 33), (E, D), jnp.float32), -6.0, 6.0) * (1.0 / math.sqrt(E))
    return matrix.astype(jnp.bfloat16)


def draw_db_states(key, part):
    states = jnp.clip(jax.random.normal(jax.random.fold_in(key, 34), (DB_ROWS, NT, E), jnp.float32), -6.0, 6.0)
    return states.astype(jnp.bfloat16)


def with_ends(drawn, own_key, least, high):
    longest = drawn.shape.index(max(drawn.shape))
    spots = []
    for shift in (0, 1):
        where = [jax.random.randint(jax.random.fold_in(own_key, axis), (), 0, length) for axis, length in enumerate(drawn.shape)]
        where[longest] = (where[longest] + shift) % drawn.shape[longest]
        spots.append(tuple(where))
    return drawn.at[spots[0]].set(least).at[spots[1]].set(high)


def shard_levels(stream_key, dims, split, smallest, top_value):
    def one(axis_at, blocks):
        draws = jax.random.uniform(jax.random.fold_in(jax.random.fold_in(stream_key, 6), axis_at), (blocks,), jnp.float32, smallest / len(split), top_value / len(split))
        return jnp.repeat(jnp.exp(draws), dims[axis_at] // blocks).reshape((-1,) + (1,) * (len(dims) - axis_at - 1))

    factor_of = one(*split[0])
    for cut in split[1:]:
        factor_of = factor_of * one(*cut)
    return factor_of


def shared_out(own_key, own, number, rows, number_of, top, most, skew):
    sequence = jax.random.permutation(own_key, number_of)
    heavy_load, ordinary = shares(number_of, rows * top, most, skew, True), shares(number_of, rows * top, most, skew, False)
    places = jnp.arange(number_of)

    def named(sizes, rotation):
        used = int((sizes > 0).sum())
        fixed = max(1, used // 4)
        shifted = fixed + (places - fixed + rotation * (used - fixed)) % max(1, number_of - fixed)
        return jnp.zeros((number_of,), jnp.int32).at[sequence[jnp.where(places < fixed, places, shifted)]].set(jnp.asarray(sizes, jnp.int32))

    sizes = jnp.where(number % 4 == 0, named(heavy_load, number // 4), named(ordinary, number - number // 4 - 1))
    mixed = jax.random.permutation(jax.random.fold_in(own, 3), number_of)
    giver, taker = mixed[0:number_of // 2 * 2:2], mixed[1:number_of // 2 * 2:2]
    room = jnp.minimum(sizes[giver] - 1, most - sizes[taker]) // 2
    room = jnp.where((giver == sequence[0]) | (taker == sequence[0]) | (sizes[taker] == 0), 0, jnp.maximum(room, 0))
    shifted = jax.random.randint(jax.random.fold_in(own, 4), (number_of // 2,), 0, 1 << 20) % (room + 1)
    sizes = sizes.at[giver].add(-shifted).at[taker].add(shifted)
    items = jnp.searchsorted(jnp.cumsum(sizes), jnp.arange(rows * top), side="right").astype(jnp.int32)
    grid = items.reshape(top, rows).T
    grid = grid[jax.random.permutation(jax.random.fold_in(own, 1), rows)]
    rotation = jax.random.randint(jax.random.fold_in(own, 2), (rows, 1), 0, top)
    return jnp.take_along_axis(grid, (jnp.arange(top)[None, :] + rotation) % top, axis=1)


def shares(number_of, total, bound, lean, full):
    weights = [(1 << 20) // math.isqrt(grade ** lean) + 1 for grade in range(1, number_of + 1)]
    largest = bound if full else min(bound, max(-(-total // number_of), total * weights[0] // sum(weights)))
    least = 1 if total - largest >= number_of - 1 else 0
    given, surplus = [largest] + [least] * (number_of - 1), total - largest - least * (number_of - 1)
    while surplus > 0:
        candidates = [i for i in range(1, number_of) if given[i] < largest] or [i for i in range(1, number_of) if given[i] < bound]
        mass, left = sum([weights[i] for i in candidates]), surplus
        for i in candidates:
            extra = min(bound - given[i], max(1, left * weights[i] // mass), surplus)
            given[i] = given[i] + extra
            surplus = surplus - extra
    return np.array(given)


def normal_values(key, extent, scale, reach, cuts=(), dtype=jnp.bfloat16):
    level = shard_levels(key, extent, cuts, -0.22, 0.18) if cuts else 1.0
    values = jax.random.normal(key, extent, jnp.float32) * scale * level
    return jnp.minimum(jnp.maximum(values, -reach), reach).astype(dtype)


def setup_inputs(seed: int = 0) -> dict:
    streams_of = jax.random.split(jax.random.key(seed), 10)
    q_self = draw_q_self(jax.random.fold_in(streams_of[9], 71), 0)
    k_self = draw_k_self(jax.random.fold_in(streams_of[9], 71), 0)
    v_self = draw_v_self(jax.random.fold_in(streams_of[9], 71), 0)
    db_states = draw_db_states(jax.random.fold_in(streams_of[9], 71), 0)
    nb_shard_keys = jax.random.split(jax.random.fold_in(streams_of[4], 1), GROUPS // GROUP_DEV)
    nb_shard_turns = jax.random.permutation(jax.random.fold_in(streams_of[4], 3), GROUPS // GROUP_DEV)
    nb_shard = jax.vmap(lambda own, number: shared_out(jax.random.fold_in(streams_of[4], 2), own, number, GROUP_DEV, N_DB, KNB, MOST, 2))(nb_shard_keys, nb_shard_turns).reshape((GROUPS, KNB))
    nb_row = with_ends(jax.random.randint(streams_of[5], (GROUPS, KNB), 0, R_DEV), jax.random.fold_in(streams_of[5], 1), 0, R_DEV - 1).astype(jnp.int32)
    wk_x = draw_wk_x(jax.random.fold_in(streams_of[9], 71), 0)
    wv_x = normal_values(streams_of[7], (E, D), E ** -0.5, 0.1875, ((1, 32),))
    wq_x = draw_wq_x(jax.random.fold_in(streams_of[9], 71), 0)
    return {"q_self": q_self, "k_self": k_self, "v_self": v_self, "db_states": db_states, "nb_shard": nb_shard, "nb_row": nb_row, "wk_x": wk_x, "wv_x": wv_x, "wq_x": wq_x}


def reference(q_self, k_self, v_self, db_states, nb_shard, nb_row, wk_x, wv_x, wq_x):
    scaling = 1.0 / math.sqrt(HD)
    query_all = q_self.reshape(SEQ, HEADS, HD).transpose(1, 0, 2)
    key_all = k_self.reshape(SEQ, HEADS, HD).transpose(1, 0, 2)
    value_all = v_self.reshape(SEQ, HEADS, HD).transpose(1, 0, 2)
    positions = jnp.arange(SEQ)
    causal = positions[:, None] >= positions[None, :]

    def one_head(operands):
        query_head, key_head, value_head = operands
        scores = jnp.dot(query_head, key_head.T, preferred_element_type=jnp.float32) * scaling
        row_max = lax.optimization_barrier(jnp.max(jnp.where(causal, scores, -1e+30), axis=1, keepdims=True))
        weights = jnp.where(causal, jnp.exp(scores - row_max), 0.0)
        denominator = lax.optimization_barrier(jnp.sum(weights, axis=1, keepdims=True))
        weighted = jnp.dot(weights.astype(jnp.bfloat16), value_head, preferred_element_type=jnp.float32)
        return (weighted / denominator).astype(jnp.bfloat16)
    self_heads = lax.map(one_head, (query_all, key_all, value_all))
    self_out = self_heads.transpose(1, 0, 2).reshape(SEQ, D)
    cross_query = jnp.dot(self_out, wq_x, preferred_element_type=jnp.float32).astype(jnp.bfloat16)
    flat_ids = (nb_shard * R_DEV + nb_row).astype(jnp.int32)
    group_query = cross_query.reshape(GROUPS, GROUP, HEADS, HD)

    def one_group(operands):
        group_ids, query_block = operands
        states = jnp.take(db_states, group_ids, axis=0).reshape(KNB * NT, E)
        nb_keys = jnp.dot(states, wk_x, preferred_element_type=jnp.float32).astype(jnp.bfloat16).reshape(KNB * NT, HEADS, HD)
        nb_values = jnp.dot(states, wv_x, preferred_element_type=jnp.float32).astype(jnp.bfloat16).reshape(KNB * NT, HEADS, HD)
        scores = jnp.einsum('qhd,khd->hqk', query_block.astype(jnp.float32), nb_keys.astype(jnp.float32)) * scaling
        row_max = lax.optimization_barrier(jnp.max(scores, axis=2, keepdims=True))
        weights = jnp.exp(scores - row_max)
        denominator = lax.optimization_barrier(jnp.sum(weights, axis=2, keepdims=True))
        weighted = jnp.einsum('hqk,khd->hqd', weights.astype(jnp.bfloat16).astype(jnp.float32), nb_values.astype(jnp.float32))
        result = (weighted / denominator).transpose(1, 0, 2).reshape(GROUP, D)
        return result.astype(jnp.bfloat16)
    cross_out = lax.map(one_group, (flat_ids, group_query)).reshape(SEQ, D)
    return (self_out, cross_out)
```

```python
import math

import jax
import jax.numpy as jnp
from jax import lax
from jax.sharding import PartitionSpec as P

HD = 128


def shifted(value, axis, steps):
    count = lax.axis_size(axis)
    initial, last = (max(0, -steps), min(count, count - steps))
    return lax.ppermute(value, axis, [(source, source + steps) for source in range(initial, last)])


def local(q_self, k_self, v_self, db_states, nb_shard, nb_row, wk_x, wv_x, wq_x):
    tok_rows = q_self.shape[0]
    head_dim = HD
    head_count = q_self.shape[1] // head_dim
    scaling = 1.0 / math.sqrt(head_dim)
    cycle_size = lax.axis_size("ctx")
    db_size = lax.axis_size("db")
    ctx_index = lax.axis_index("ctx")
    db_index = lax.axis_index("db")
    query_heads = q_self.reshape(tok_rows, head_count, head_dim)
    query_pos = ctx_index * tok_rows + jnp.arange(tok_rows)
    initial = (
        jnp.full((head_count, tok_rows, 1), -1e30, jnp.float32),
        jnp.zeros((head_count, tok_rows, 1), jnp.float32),
        jnp.zeros((head_count, tok_rows, head_dim), jnp.float32),
    )
    state_now = initial
    stacked = jnp.stack([k_self, v_self])
    for turn_index in range(cycle_size):
        source = ctx_index - turn_index
        key_block = stacked[0]
        attend_row_max, attend_denominator, attend_numerator = state_now
        row_count = key_block.shape[0]
        key_heads = key_block.reshape(row_count, head_count, head_dim)
        value_heads = stacked[1].reshape(row_count, head_count, head_dim)
        attend_scores = (
            jnp.einsum("qhd,khd->hqk", query_heads, key_heads, preferred_element_type=jnp.float32)
            * scaling
        )
        key_pos = source * tok_rows + jnp.arange(row_count)
        allowed = ((query_pos[:, None] >= key_pos[None, :]) & (key_pos[None, :] >= 0))[None]
        max_next = jnp.maximum(
            attend_row_max, jnp.max(jnp.where(allowed, attend_scores, -1e30), axis=2, keepdims=True)
        )
        attend_weights = jnp.where(allowed, jnp.exp(attend_scores - max_next), 0.0)
        factor = jnp.exp(attend_row_max - max_next)
        attend_denominator = attend_denominator * factor + jnp.sum(
            attend_weights, axis=2, keepdims=True
        )
        attend_numerator = attend_numerator * factor + jnp.einsum(
            "hqk,khd->hqd",
            attend_weights.astype(jnp.bfloat16),
            value_heads,
            preferred_element_type=jnp.float32,
        )
        state_now = (max_next, attend_denominator, attend_numerator)
        if turn_index + 1 < cycle_size:
            stacked = shifted(stacked, "ctx", 1)
    row_max, denominator, numerator = state_now
    self_out = (
        (numerator / denominator)
        .transpose(1, 0, 2)
        .reshape(tok_rows, head_count * head_dim)
        .astype(jnp.bfloat16)
    )
    cross_query = jnp.dot(
        lax.all_gather(self_out, "db", axis=1, tiled=True), wq_x, preferred_element_type=jnp.float32
    ).astype(jnp.bfloat16)
    group_count = nb_shard.shape[0]
    per_group = nb_shard.shape[1]
    requests = group_count * per_group
    capacity = 2 * ((requests + db_size - 1) // db_size)
    shard_flat = nb_shard.reshape(requests)
    row_flat = nb_row.reshape(requests)
    same_shard = shard_flat[:, None] == shard_flat[None, :]
    earlier = jnp.arange(requests)[None, :] < jnp.arange(requests)[:, None]
    rank_within = jnp.sum((same_shard & earlier).astype(jnp.int32), axis=1)
    picked = (shard_flat[None, :] == db_index) & (
        rank_within[None, :] == jnp.arange(capacity)[:, None]
    )
    slot_rows = jnp.sum(jnp.where(picked, row_flat[None, :], 0), axis=1)
    slot_states = jnp.concatenate([lax.dynamic_slice_in_dim(db_states, slot_rows[i], 1, 0) for i in range(capacity)], axis=0)
    state_len = db_states.shape[1]
    state_width = db_states.shape[2]
    slot_of = shard_flat * capacity + rank_within
    gathered = lax.all_gather(slot_states, "db", axis=0, tiled=True)
    requested = jnp.concatenate([lax.dynamic_slice_in_dim(gathered, slot_of[i], 1, 0) for i in range(requests)], axis=0)
    flat_states = requested.reshape(requests * state_len, state_width)
    nb_keys = (
        jnp.dot(flat_states, wk_x, preferred_element_type=jnp.float32)
        .astype(jnp.bfloat16)
        .reshape(requests, state_len, head_count, head_dim)
    )
    nb_values = (
        jnp.dot(flat_states, wv_x, preferred_element_type=jnp.float32)
        .astype(jnp.bfloat16)
        .reshape(requests, state_len, head_count, head_dim)
    )
    chosen = jnp.concatenate([nb_keys, nb_values], axis=3).reshape(
        group_count, per_group * state_len, head_count, 2 * head_dim
    )
    group_keys = chosen[..., :head_dim]
    group_values = chosen[..., head_dim:]
    group_len = tok_rows // group_count
    group_query = cross_query.reshape(group_count, group_len, head_count, head_dim)
    scores = (
        jnp.einsum("cqhd,ckhd->chqk", group_query, group_keys, preferred_element_type=jnp.float32)
        * scaling
    )
    cross_max = jnp.max(scores, axis=3, keepdims=True)
    weights = jnp.exp(scores - cross_max)
    cross_total = jnp.sum(weights, axis=3, keepdims=True)
    weighted = jnp.einsum(
        "chqk,ckhd->chqd",
        weights.astype(jnp.bfloat16),
        group_values,
        preferred_element_type=jnp.float32,
    )
    cross_out = (
        (weighted / cross_total)
        .transpose(0, 2, 1, 3)
        .reshape(tok_rows, head_count * head_dim)
        .astype(jnp.bfloat16)
    )
    return (self_out, cross_out)


def solution(mesh):
    return jax.shard_map(
        local,
        mesh=mesh,
        in_specs=(
            P("ctx", "db"),
            P("ctx", "db"),
            P("ctx", "db"),
            P("db", None, None),
            P("ctx", None),
            P("ctx", None),
            P(None, "db"),
            P(None, "db"),
            P(None, "db"),
        ),
        out_specs=(P("ctx", "db"), P("ctx", "db")),
        check_vma=False,
    )
```

```python
import functools
import math

import jax
import jax.numpy as jnp
from jax import lax
from jax.experimental import pallas as pl
from jax.experimental.pallas import tpu as pltpu
from jax.sharding import Mesh
from jax.sharding import PartitionSpec as P

HD = 128
AXES = ("x_hi", "y", "z", "x_lo", "core")
CTX = ("x_hi", "y")
DB = ("z", "x_lo", "core")
XC = ("x_lo", "core")
XX = ("x_hi", "x_lo")
LOW = -1e30
EXP2_SCALE = math.log2(math.e) / math.sqrt(HD)
BF = jnp.bfloat16
F32 = jnp.float32


def ring(value, axis, step):
    n = lax.axis_size(axis)
    return lax.ppermute(value, axis, [(i, (i + step) % n) for i in range(n)])


def swap(value, axis):
    return lax.ppermute(value, axis, [(0, 1), (1, 0)])


def params(megabytes):
    return pltpu.CompilerParams(
        dimension_semantics=("arbitrary",), vmem_limit_bytes=megabytes << 20
    )


def dot_t(a, b):
    return lax.dot_general(a, b, (((1,), (1,)), ((), ())), preferred_element_type=F32)


def attend_kernel(
    tile, flags, q_ref, qs_ref, kv0, kv1, kv2, k3, v3, o_ref, lse_ref, os_ref, lses_ref, kx, vx, m_ref, acc
):
    t = pl.program_id(0)
    rows = kx.shape[1]
    tiles = rows // tile

    @pl.when(t == 0)
    def _():
        for b, (key, value) in enumerate(
            ((kv0.at[0], kv0.at[1]), (kv1.at[0], kv1.at[1]), (kv2.at[0], kv2.at[1]), (k3, v3))
        ):
            kx[b] = key[...]
            vx[b, :, :HD] = value[...]
            vx[b, :, HD:] = jnp.ones((rows, HD), BF)

    def step(q, b, masked):
        s = dot_t(q, kx[b])
        if masked:
            row = lax.broadcasted_iota(jnp.int32, s.shape, 0) + t * tile
            s = jnp.where(row >= lax.broadcasted_iota(jnp.int32, s.shape, 1), s, LOW)
        before = m_ref[...]
        now = jnp.maximum(before, jnp.max(s, axis=1, keepdims=True))
        p = jnp.exp2((s - now[:, :1]) * EXP2_SCALE)
        factor = jnp.exp2((before - now) * EXP2_SCALE)
        m_ref[...] = now
        acc[...] = acc[...] * jnp.concatenate([factor, factor], axis=1) + jnp.dot(
            p.astype(BF), vx[b], preferred_element_type=F32
        )

    def finish():
        total = acc[:, HD:]
        lse = m_ref[...] * EXP2_SCALE + jnp.log2(total)
        return acc[:, :HD] / total, lse.T[:1]

    m_ref[...] = jnp.full_like(m_ref, LOW)
    acc[...] = jnp.zeros_like(acc)

    @pl.when(t < tiles)
    def _():
        q = q_ref[...]
        step(q, 0, True)

        @pl.loop(1, 4)
        def _(b):
            @pl.when(flags[b] == 1)
            def _():
                step(q, b, False)

        o, lse = finish()
        o_ref[...] = o
        lse_ref[0] = lse

    @pl.when((t >= tiles) & (flags[0] == 1))
    def _():
        q = qs_ref[...]

        @pl.loop(0, 4)
        def _(b):
            step(q, b, False)

        o, lse = finish()
        os_ref[...] = o.astype(BF)
        lses_ref[0] = lse


def attend(flags, q, qs, kv0, kv1, kv2, k3, v3):
    rows = q.shape[0]
    tile = 256
    tiles = rows // tile
    first = lambda t, f: (jnp.minimum(t, tiles - 1), 0)
    second = lambda t, f: (jnp.maximum(t - tiles, 0), 0)
    whole3 = pl.BlockSpec((2, rows, HD), lambda t, f: (0, 0, 0))
    whole2 = pl.BlockSpec((rows, HD), lambda t, f: (0, 0))
    stat = jax.ShapeDtypeStruct((tiles, 1, tile), F32)
    return pl.pallas_call(
        functools.partial(attend_kernel, tile),
        grid_spec=pltpu.PrefetchScalarGridSpec(
            num_scalar_prefetch=1,
            grid=(2 * tiles,),
            in_specs=[
                pl.BlockSpec((tile, HD), first),
                pl.BlockSpec((tile, HD), second),
                whole3,
                whole3,
                whole3,
                whole2,
                whole2,
            ],
            out_specs=[
                pl.BlockSpec((tile, HD), first),
                pl.BlockSpec((1, 1, tile), lambda t, f: (jnp.minimum(t, tiles - 1), 0, 0)),
                pl.BlockSpec((tile, HD), second),
                pl.BlockSpec((1, 1, tile), lambda t, f: (jnp.maximum(t - tiles, 0), 0, 0)),
            ],
            scratch_shapes=[
                pltpu.VMEM((4, rows, HD), BF),
                pltpu.VMEM((4, rows, 2 * HD), BF),
                pltpu.VMEM((tile, HD), F32),
                pltpu.VMEM((tile, 2 * HD), F32),
            ],
        ),
        out_shape=[
            jax.ShapeDtypeStruct((rows, HD), F32),
            stat,
            jax.ShapeDtypeStruct((rows, HD), BF),
            stat,
        ],
        compiler_params=params(40),
        cost_estimate=pl.CostEstimate(flops=3 << 30, bytes_accessed=4 << 20, transcendentals=0),
        name="attend",
    )(flags, q, qs, kv0, kv1, kv2, k3, v3)


def pick_rows(states, rows):
    return jnp.concatenate([lax.dynamic_slice_in_dim(states, rows[i], 1, 0) for i in range(rows.shape[0])], axis=0)


def cross_queries(z, parts, weights):
    total = 0.0
    for back, part in enumerate(parts):
        a = part.transpose(1, 0, 2).reshape(part.shape[1], -1)
        w = lax.dynamic_index_in_dim(weights, (z + 8 - back) % 8, 0, keepdims=False)
        total = total + jnp.dot(a, w, preferred_element_type=F32)
    return total.astype(BF)


def cross(slots, gathered, wk4, wv4, queries):
    picked = jnp.concatenate([lax.dynamic_slice_in_dim(gathered, slots[i], 1, 0) for i in range(slots.shape[0])], axis=0)
    picked = picked.reshape(-1, picked.shape[2])
    keys = jnp.dot(picked, wk4, preferred_element_type=F32).astype(BF).reshape(4, -1, 4, HD)
    values = jnp.dot(picked, wv4, preferred_element_type=F32).astype(BF).reshape(4, -1, 4, HD)
    q = queries.reshape(4, -1, 4, HD)
    scores = jnp.einsum("cqhd,ckhd->chqk", q, keys, preferred_element_type=F32)
    p = jnp.exp2((scores - jnp.max(scores, axis=3, keepdims=True)) * EXP2_SCALE)
    total = jnp.sum(p, axis=3, keepdims=True)
    o = jnp.einsum("chqk,ckhd->chqd", p.astype(BF), values, preferred_element_type=F32) / total
    o = o.astype(BF).transpose(1, 0, 2, 3).reshape(4, -1, HD)
    o = jnp.where(lax.axis_index("x_lo") == 1, jnp.concatenate([o[2:], o[:2]]), o)
    return jnp.where(lax.axis_index("core") == 1, jnp.stack([o[1], o[0], o[3], o[2]]), o)


def local(q, k, v, states, nb_shard, nb_row, wk, wv, wq):
    rows = q.shape[0]
    y = lax.axis_index("y")
    z = lax.axis_index("z")
    late = lax.axis_index("x_hi") == 1
    xc = lax.axis_index(XC)
    db_index = lax.axis_index(DB)
    db_size = lax.axis_size(DB)

    requests = nb_shard.size
    capacity = 2 * ((requests + db_size - 1) // db_size)
    shard_flat = nb_shard.reshape(requests)
    row_flat = nb_row.reshape(requests)
    same = shard_flat[:, None] == shard_flat[None, :]
    earlier = jnp.arange(requests)[None, :] < jnp.arange(requests)[:, None]
    rank = jnp.sum((same & earlier).astype(jnp.int32), axis=1)
    picked = (shard_flat[None, :] == db_index) & (rank[None, :] == jnp.arange(capacity)[:, None])
    slot_rows = jnp.sum(jnp.where(picked, row_flat[None, :], 0), axis=1)
    slot_of = shard_flat * capacity + rank
    gathered = lax.all_gather(pick_rows(states, slot_rows), DB, axis=0, tiled=True)

    kv0 = jnp.stack([k, v])
    kv1 = ring(kv0, "y", 1)
    kv2 = ring(kv0, "y", -1)
    qs = lax.ppermute(q, "x_hi", [(1, 0)])
    k3 = ring(kv1[0], "y", 1)
    v3 = ring(kv2[1], "y", -1)
    flags = jnp.stack([~late, y >= 1, y >= 3, y >= 2]).astype(jnp.int32)
    o, lse, o_sent, lse_sent = attend(flags, q, qs, kv0, kv1, kv2, k3, v3)
    o_back = lax.ppermute(o_sent, "x_hi", [(0, 1)])
    lse_back = lax.ppermute(lse_sent, "x_hi", [(0, 1)])
    lse_own = lse.reshape(rows, 1)
    lse_back = jnp.where(late, lse_back.reshape(rows, 1), LOW)
    top = jnp.maximum(lse_own, lse_back)
    e_own = jnp.exp2(lse_own - top)
    e_back = jnp.exp2(lse_back - top)
    self_out = ((o * e_own + o_back.astype(F32) * e_back) / (e_own + e_back)).astype(BF)

    wall = jnp.concatenate([wq, wk, wv], axis=0)
    half = wall.shape[0] // 2
    w_x = jnp.concatenate([ring(wall[:half], XX, -1), ring(wall[half:], XX, 1)], axis=0)
    w4 = jnp.concatenate([wall, swap(wall, "core"), w_x, swap(w_x, "core")], axis=1)
    depth, width = wq.shape[0], wk.shape[0]
    wq4 = w4[:depth].reshape(8, depth // 8, 4 * HD)
    wk4 = w4[depth : depth + width]
    wv4 = w4[depth + width :]

    mine = lax.all_to_all(self_out.reshape(4, rows // 4, HD), XC, 0, 0)
    f1 = ring(mine, "z", 1)
    b1 = ring(mine, "z", -1)
    f2 = ring(f1, "z", 1)
    b2 = ring(b1, "z", -1)
    f3 = ring(f2, "z", 1)
    b3 = ring(b2, "z", -1)
    far = jnp.concatenate([ring(f3[:2], "z", 1), ring(b3[2:], "z", -1)], axis=0)
    queries = cross_queries(z, (mine, f1, f2, f3, far, b3, b2, b1), wq4)

    per = requests // 4
    slots = lax.dynamic_slice(slot_of, (xc * per,), (per,))
    out = cross(slots, gathered, wk4, wv4, queries)
    cross_out = lax.all_to_all(out, XC, 0, 0).reshape(rows, HD)
    return (self_out, cross_out)


def solution(mesh):
    fine = Mesh(mesh.devices.reshape(2, 4, 8, 2, 2), AXES)
    return jax.shard_map(
        local,
        mesh=fine,
        in_specs=(
            P(CTX, DB),
            P(CTX, DB),
            P(CTX, DB),
            P(DB, None, None),
            P(CTX, None),
            P(CTX, None),
            P(None, DB),
            P(None, DB),
            P(None, DB),
        ),
        out_specs=(P(CTX, DB), P(CTX, DB)),
        check_vma=False,
    )
```

```python
import functools
import math

import jax
import jax.numpy as jnp
from jax import lax
from jax.experimental import pallas as pl
from jax.experimental.pallas import tpu as pltpu
from jax.sharding import Mesh
from jax.sharding import PartitionSpec as P

HD = 128
AXES = ("x_hi", "y", "z", "x_lo", "core")
CTX = ("x_hi", "y")
DB = ("z", "x_lo", "core")
XC = ("x_lo", "core")
XX = ("x_hi", "x_lo")
LOW = -1e30
EXP2_SCALE = math.log2(math.e) / math.sqrt(HD)
BF = jnp.bfloat16
F32 = jnp.float32


def ring(value, axis, step):
    n = lax.axis_size(axis)
    return lax.ppermute(value, axis, [(i, (i + step) % n) for i in range(n)])


def swap(value, axis):
    return lax.ppermute(value, axis, [(0, 1), (1, 0)])


def params(megabytes):
    return pltpu.CompilerParams(
        dimension_semantics=("arbitrary",), vmem_limit_bytes=megabytes << 20
    )


def dot_t(a, b):
    return lax.dot_general(a, b, (((1,), (1,)), ((), ())), preferred_element_type=F32)


def attend_kernel(
    tile, flags, q_ref, qs_ref, kv0, kv1, kv2, k3, v3, o_ref, lse_ref, os_ref, lses_ref, kx, vx, m_ref, acc
):
    t = pl.program_id(0)
    rows = kx.shape[1]
    tiles = rows // tile

    @pl.when(t == 0)
    def _():
        for b, (key, value) in enumerate(
            ((kv0.at[0], kv0.at[1]), (kv1.at[0], kv1.at[1]), (kv2.at[0], kv2.at[1]), (k3, v3))
        ):
            kx[b] = key[...]
            vx[b, :, :HD] = value[...]
            vx[b, :, HD:] = jnp.ones((rows, HD), BF)

    def step(q, b, masked):
        s = dot_t(q, kx[b])
        if masked:
            row = lax.broadcasted_iota(jnp.int32, s.shape, 0) + t * tile
            s = jnp.where(row >= lax.broadcasted_iota(jnp.int32, s.shape, 1), s, LOW)
        before = m_ref[...]
        now = jnp.maximum(before, jnp.max(s, axis=1, keepdims=True))
        p = jnp.exp2((s - now[:, :1]) * EXP2_SCALE)
        factor = jnp.exp2((before - now) * EXP2_SCALE)
        m_ref[...] = now
        acc[...] = acc[...] * jnp.concatenate([factor, factor], axis=1) + jnp.dot(
            p.astype(BF), vx[b], preferred_element_type=F32
        )

    def finish():
        total = acc[:, HD:]
        lse = m_ref[...] * EXP2_SCALE + jnp.log2(total)
        return acc[:, :HD] / total, lse.T[:1]

    m_ref[...] = jnp.full_like(m_ref, LOW)
    acc[...] = jnp.zeros_like(acc)

    @pl.when(t < tiles)
    def _():
        q = q_ref[...]
        step(q, 0, True)

        @pl.loop(1, 4)
        def _(b):
            @pl.when(flags[b] == 1)
            def _():
                step(q, b, False)

        o, lse = finish()
        o_ref[...] = o
        lse_ref[0] = lse

    @pl.when((t >= tiles) & (flags[0] == 1))
    def _():
        q = qs_ref[...]

        @pl.loop(0, 4)
        def _(b):
            step(q, b, False)

        o, lse = finish()
        os_ref[...] = o.astype(BF)
        lses_ref[0] = lse


def attend(flags, q, qs, kv0, kv1, kv2, k3, v3):
    rows = q.shape[0]
    tile = 256
    tiles = rows // tile
    first = lambda t, f: (jnp.minimum(t, tiles - 1), 0)
    second = lambda t, f: (jnp.maximum(t - tiles, 0), 0)
    whole3 = pl.BlockSpec((2, rows, HD), lambda t, f: (0, 0, 0))
    whole2 = pl.BlockSpec((rows, HD), lambda t, f: (0, 0))
    stat = jax.ShapeDtypeStruct((tiles, 1, tile), F32)
    return pl.pallas_call(
        functools.partial(attend_kernel, tile),
        grid_spec=pltpu.PrefetchScalarGridSpec(
            num_scalar_prefetch=1,
            grid=(2 * tiles,),
            in_specs=[
                pl.BlockSpec((tile, HD), first),
                pl.BlockSpec((tile, HD), second),
                whole3,
                whole3,
                whole3,
                whole2,
                whole2,
            ],
            out_specs=[
                pl.BlockSpec((tile, HD), first),
                pl.BlockSpec((1, 1, tile), lambda t, f: (jnp.minimum(t, tiles - 1), 0, 0)),
                pl.BlockSpec((tile, HD), second),
                pl.BlockSpec((1, 1, tile), lambda t, f: (jnp.maximum(t - tiles, 0), 0, 0)),
            ],
            scratch_shapes=[
                pltpu.VMEM((4, rows, HD), BF),
                pltpu.VMEM((4, rows, 2 * HD), BF),
                pltpu.VMEM((tile, HD), F32),
                pltpu.VMEM((tile, 2 * HD), F32),
            ],
        ),
        out_shape=[
            jax.ShapeDtypeStruct((rows, HD), F32),
            stat,
            jax.ShapeDtypeStruct((rows, HD), BF),
            stat,
        ],
        compiler_params=params(40),
        cost_estimate=pl.CostEstimate(flops=3 << 30, bytes_accessed=4 << 20, transcendentals=0),
        name="attend",
    )(flags, q, qs, kv0, kv1, kv2, k3, v3)


def cross_queries(z, parts, weights):
    total = 0.0
    for back, part in parts:
        a = jnp.concatenate([part[h] for h in range(part.shape[0])], axis=1)
        w = lax.dynamic_index_in_dim(weights, (z + 8 - back) % 8, 0, keepdims=False)
        total = total + jnp.dot(a, w, preferred_element_type=F32)
    return total


def project_kernel(s_ref, w_ref, out):
    a = s_ref[...].reshape(-1, s_ref.shape[2])
    out[...] = jnp.dot(a, w_ref[...], preferred_element_type=F32).astype(BF).reshape(out.shape)


def project(slots, weights):
    n, length, width = slots.shape
    columns = weights.shape[1]
    return pl.pallas_call(
        project_kernel,
        grid=(n // 2,),
        in_specs=[
            pl.BlockSpec((2, length, width), lambda i: (i, 0, 0)),
            pl.BlockSpec(weights.shape, lambda i: (0, 0)),
        ],
        out_specs=pl.BlockSpec((2, length, columns), lambda i: (i, 0, 0)),
        out_shape=jax.ShapeDtypeStruct((n, length, columns), BF),
        compiler_params=params(24),
        cost_estimate=pl.CostEstimate(flops=4 << 30, bytes_accessed=10 << 20, transcendentals=0),
        name="project",
    )(slots, weights)


def cross_kernel(info, qa_ref, qb_ref, kva, kvb, o_ref, lse_ref, m_ref, l_ref, acc):
    g = pl.program_id(0)
    half = pl.num_programs(0) // 2
    slots = kva.shape[0]
    m_ref[...] = jnp.full_like(m_ref, LOW)
    l_ref[...] = jnp.zeros_like(l_ref)
    acc[...] = jnp.zeros_like(acc)
    q = jnp.where(g < half, qa_ref[...], qb_ref[...])

    def attend_slot(kv):
        for r in range(4):
            cut = slice(r * HD, (r + 1) * HD)
            s = dot_t(q[:, cut], kv[:, cut])
            before = m_ref[r]
            now = jnp.maximum(before, jnp.max(s, axis=1, keepdims=True))
            p = jnp.exp2((s - now) * EXP2_SCALE)
            factor = jnp.exp2((before - now) * EXP2_SCALE)
            m_ref[r] = now
            l_ref[r] = l_ref[r] * factor + jnp.sum(p, axis=1, keepdims=True)
            acc[r] = acc[r] * factor + jnp.dot(
                p.astype(BF), kv[:, 4 * HD + r * HD : 4 * HD + (r + 1) * HD], preferred_element_type=F32
            )

    for n in range(2):
        slot = info[2 * g + n]

        @pl.when((slot >= 0) & (slot < slots))
        def _():
            attend_slot(kva[slot])

        @pl.when(slot >= slots)
        def _():
            attend_slot(kvb[slot - slots])

    lane = lax.broadcasted_iota(jnp.int32, acc.shape[1:], 1)
    stats = jnp.full(acc.shape[1:], LOW, F32)
    for r in range(4):
        total = l_ref[r]
        some = total > 0
        safe = jnp.where(some, total, 1.0)
        o_ref[r] = (acc[r] / safe).astype(BF)
        stats = jnp.where((lane == r) & some, m_ref[r] * EXP2_SCALE + jnp.log2(safe), stats)
    lse_ref[0] = stats.T[:8]


def cross(info, queries_a, queries_b, kva, kvb):
    groups = 8
    group = queries_a.shape[0] // 4
    width = queries_a.shape[1]
    whole = pl.BlockSpec(kva.shape, lambda g, s: (0, 0, 0))
    return pl.pallas_call(
        cross_kernel,
        grid_spec=pltpu.PrefetchScalarGridSpec(
            num_scalar_prefetch=1,
            grid=(groups,),
            in_specs=[
                pl.BlockSpec((group, width), lambda g, s: (jnp.minimum(g, 3), 0)),
                pl.BlockSpec((group, width), lambda g, s: (jnp.maximum(g - 4, 0), 0)),
                whole,
                whole,
            ],
            out_specs=[
                pl.BlockSpec((4, group, HD), lambda g, s: (0, g, 0)),
                pl.BlockSpec((1, 8, group), lambda g, s: (g, 0, 0)),
            ],
            scratch_shapes=[
                pltpu.VMEM((4, group, HD), F32),
                pltpu.VMEM((4, group, HD), F32),
                pltpu.VMEM((4, group, HD), F32),
            ],
        ),
        out_shape=[
            jax.ShapeDtypeStruct((4, groups * group, HD), BF),
            jax.ShapeDtypeStruct((groups, 8, group), F32),
        ],
        compiler_params=params(40),
        cost_estimate=pl.CostEstimate(flops=1 << 30, bytes_accessed=9 << 20, transcendentals=0),
        name="cross",
    )(info, queries_a, queries_b, kva, kvb)


def merge(o_a, lse_a, o_b, lse_b):
    top = jnp.maximum(lse_a, lse_b)
    e_a = jnp.exp2(lse_a - top)
    e_b = jnp.exp2(lse_b - top)
    return ((o_a.astype(F32) * e_a + o_b.astype(F32) * e_b) / (e_a + e_b)).astype(BF)


def local(q, k, v, states, nb_shard, nb_row, wk, wv, wq):
    rows = q.shape[0]
    quarter = rows // 4
    y = lax.axis_index("y")
    z = lax.axis_index("z")
    x_lo = lax.axis_index("x_lo")
    core = lax.axis_index("core")
    late = lax.axis_index("x_hi") == 1
    db_index = lax.axis_index(DB)

    place = 2 * lax.broadcasted_iota(jnp.int32, nb_shard.shape, 0) + lax.broadcasted_iota(
        jnp.int32, nb_shard.shape, 1
    )
    coded = place * states.shape[0] + nb_row
    asked = nb_shard == db_index
    none = nb_shard.size * states.shape[0]
    first = jnp.min(jnp.where(asked, coded, none)) % states.shape[0]
    last = jnp.max(jnp.where(asked, coded, 0)) % states.shape[0]
    pair = jnp.concatenate(
        [lax.dynamic_slice_in_dim(states, i, 1, 0) for i in (first, last)], axis=0
    )
    held_a = lax.all_gather(pair, "z", axis=0, tiled=True)

    kv0 = jnp.stack([k, v])
    kv1 = ring(kv0, "y", 1)
    kv2 = ring(kv0, "y", -1)
    qs = lax.ppermute(q, "x_hi", [(1, 0)])
    k3 = ring(kv1[0], "y", 1)
    v3 = ring(kv2[1], "y", -1)
    flags = jnp.stack([~late, y >= 1, y >= 3, y >= 2]).astype(jnp.int32)
    wall = jnp.concatenate([wq, wk, wv], axis=0)
    half = wall.shape[0] // 2
    w_up = ring(wall[:half], XX, -1)
    w_down = ring(wall[half:], XX, 1)
    o, lse, o_sent, lse_sent = attend(flags, q, qs, kv0, kv1, kv2, k3, v3)

    o_sent, lse_sent, w_up, w_down = lax.optimization_barrier((o_sent, lse_sent, w_up, w_down))
    o_back = lax.ppermute(o_sent, "x_hi", [(0, 1)])
    lse_back = lax.ppermute(lse_sent, "x_hi", [(0, 1)])
    w_x = jnp.concatenate([w_up, w_down], axis=0)
    w4 = jnp.concatenate([wall, swap(wall, "core"), w_x, swap(w_x, "core")], axis=1)
    depth, width = wq.shape[0], wk.shape[0]
    wq4 = w4[:depth].reshape(8, depth // 8, 4 * HD)
    wkv4 = jnp.concatenate([w4[depth : depth + width], w4[depth + width :]], axis=1)
    o_back, lse_back, wq4, wkv4 = lax.optimization_barrier((o_back, lse_back, wq4, wkv4))

    lse_back = jnp.where(late, lse_back.reshape(rows, 1), LOW)
    self_out = merge(o, lse.reshape(rows, 1), o_back, lse_back)

    mine = lax.all_to_all(self_out.reshape(4, quarter, HD), XC, 0, 0)
    f1 = ring(mine, "z", 1)
    b1 = ring(mine, "z", -1)
    f2 = ring(f1, "z", 1)
    b2 = ring(b1, "z", -1)
    held_b = swap(held_a, "core")
    f3 = ring(f2, "z", 1)
    b3 = ring(b2, "z", -1)
    far_f = ring(f3[:2], "z", 1)
    far_b = ring(b3[2:], "z", -1)
    near = cross_queries(
        z, ((0, mine), (1, f1), (2, f2), (3, f3), (5, b3), (6, b2), (7, b1)), wq4
    )
    kva = project(held_a, wkv4)
    kvb = project(held_b, wkv4)
    far_f, far_b, near, kva, kvb = lax.optimization_barrier((far_f, far_b, near, kva, kvb))
    far = jnp.concatenate([far_f, far_b], axis=0)
    queries = (near + cross_queries(z, ((4, far),), wq4)).astype(BF)

    other = swap(queries, "x_lo")
    other = jnp.concatenate([other[:, 2 * HD :], other[:, : 2 * HD]], axis=1)
    same = nb_shard.reshape(-1)[:, None] == nb_shard.reshape(-1)[None, :]
    n = nb_shard.size
    before = lax.broadcasted_iota(jnp.int32, (n, n), 1) < lax.broadcasted_iota(jnp.int32, (n, n), 0)
    rank = jnp.max((same & before).astype(jnp.int32), axis=1)
    shard = nb_shard.reshape(-1)
    slot = ((shard % 2) ^ core) * 16 + (shard // 4) * 2 + rank
    slot = jnp.where((shard // 2) % 2 == x_lo, slot, -1).reshape(4, n // 4)
    info = jnp.concatenate(
        [
            lax.dynamic_slice_in_dim(slot, 2 * x_lo + core, 1, 0),
            lax.dynamic_slice_in_dim(slot, 2 * (1 - x_lo) + core, 1, 0),
        ],
        axis=1,
    ).reshape(-1)
    o, lse = cross(info, queries, other, kva, kvb)

    lse = lse[:, :4].transpose(1, 0, 2).reshape(4, 2, 2 * HD)
    o_got = swap(o[2:], "x_lo").reshape(2, 2, quarter, HD)[:, ::-1]
    lse_got = swap(lse[2:], "x_lo")[:, ::-1]
    both = merge(
        o[:2].reshape(2, 2, quarter, HD), lse[:2][..., None], o_got, lse_got[..., None]
    )
    kept, got = both[0], swap(both[1], "core")
    kept, got = (jnp.where(x_lo == 0, a, a[::-1]) for a in (kept, got))
    cross_out = jnp.where(
        core == 0, jnp.stack([kept, got], axis=1), jnp.stack([got, kept], axis=1)
    ).reshape(rows, HD)
    return (self_out, cross_out)


def solution(mesh):
    fine = Mesh(mesh.devices.reshape(2, 4, 8, 2, 2), AXES)
    return jax.shard_map(
        local,
        mesh=fine,
        in_specs=(
            P(CTX, DB),
            P(CTX, DB),
            P(CTX, DB),
            P(DB, None, None),
            P(CTX, None),
            P(CTX, None),
            P(None, DB),
            P(None, DB),
            P(None, DB),
        ),
        out_specs=(P(CTX, DB), P(CTX, DB)),
        check_vma=False,
    )
```

```python
import functools
import math

import jax
import jax.numpy as jnp
from jax import lax
from jax.experimental import pallas as pl
from jax.experimental.pallas import tpu as pltpu
from jax.sharding import Mesh
from jax.sharding import PartitionSpec as P

HD = 128
AXES = ("x_hi", "y", "z", "x_lo", "core")
CTX = ("x_hi", "y")
DB = ("z", "x_lo", "core")
XC = ("x_lo", "core")
XX = ("x_hi", "x_lo")
LOW = -1e30
EXP2_SCALE = math.log2(math.e) / math.sqrt(HD)
BF = jnp.bfloat16
F32 = jnp.float32


def ring(value, axis, step):
    n = lax.axis_size(axis)
    return lax.ppermute(value, axis, [(i, (i + step) % n) for i in range(n)])


def swap(value, axis):
    return lax.ppermute(value, axis, [(0, 1), (1, 0)])


def params(megabytes):
    return pltpu.CompilerParams(
        dimension_semantics=("arbitrary",), vmem_limit_bytes=megabytes << 20
    )


def dot_t(a, b):
    return lax.dot_general(a, b, (((1,), (1,)), ((), ())), preferred_element_type=F32)


SUB = 256


def load_block(kx, vx, key, value):
    kx[...] = key.T
    vx[:, :HD] = value
    vx[:, HD:] = jnp.ones_like(value)


def absorb(q_ref, kx, vx, m_ref, acc):
    def scores(i):
        return jnp.dot(q_ref[i * SUB : (i + 1) * SUB, :], kx[...], preferred_element_type=F32)

    n = q_ref.shape[0] // SUB
    s = scores(0)
    for i in range(n):
        ahead = scores(i + 1) if i + 1 < n else None
        r = slice(i * SUB, (i + 1) * SUB)
        before = m_ref[r]
        now = jnp.maximum(before, jnp.max(s, axis=1, keepdims=True))
        p = jnp.exp2((s - now[:, :1]) * EXP2_SCALE)
        factor = jnp.exp2((before - now) * EXP2_SCALE)
        m_ref[r] = now
        acc[r] = acc[r] * jnp.concatenate([factor, factor], axis=1) + jnp.dot(
            p.astype(BF), vx[...], preferred_element_type=F32
        )
        s = ahead


def own_kernel(q_ref, kv_ref, m_ref, acc, kx, vx):
    load_block(kx, vx, kv_ref[0], kv_ref[1])

    def scores(i):
        seen = (i + 1) * SUB
        s = jnp.dot(q_ref[i * SUB : seen, :], kx[:, :seen], preferred_element_type=F32)
        row = lax.broadcasted_iota(jnp.int32, s.shape, 0) + i * SUB
        return jnp.where(row >= lax.broadcasted_iota(jnp.int32, s.shape, 1), s, LOW)

    n = q_ref.shape[0] // SUB
    s = scores(0)
    for i in range(n):
        ahead = scores(i + 1) if i + 1 < n else None
        r = slice(i * SUB, (i + 1) * SUB)
        now = jnp.max(s, axis=1, keepdims=True)
        p = jnp.exp2((s - now) * EXP2_SCALE)
        m_ref[r] = jnp.broadcast_to(now, (SUB, HD))
        acc[r] = jnp.dot(p.astype(BF), vx[: (i + 1) * SUB, :], preferred_element_type=F32)
        s = ahead


def attend_own(q, kv):
    rows = q.shape[0]
    return pl.pallas_call(
        own_kernel,
        in_specs=[pl.BlockSpec(memory_space=pltpu.VMEM)] * 2,
        out_specs=[pl.BlockSpec(memory_space=pltpu.VMEM)] * 2,
        out_shape=[jax.ShapeDtypeStruct((rows, HD), F32), jax.ShapeDtypeStruct((rows, 2 * HD), F32)],
        scratch_shapes=[pltpu.VMEM((HD, rows), BF), pltpu.VMEM((rows, 2 * HD), BF)],
        compiler_params=pltpu.CompilerParams(vmem_limit_bytes=24 << 20),
        cost_estimate=pl.CostEstimate(flops=1 << 30, bytes_accessed=3 << 20, transcendentals=0),
        name="attend_own",
    )(q, kv)


def middle_kernel(flags, q_ref, qs_ref, m_in, acc_in, kv0, kv1, kv2, m_ref, acc, qx, kx, vx):
    which = pl.program_id(0)

    @pl.when(which == 0)
    def _():
        for b, kv in enumerate((kv0, kv1, kv2)):
            load_block(kx.at[b], vx.at[b], kv[0], kv[1])
        qx[...] = q_ref[...]
        m_ref[0] = m_in[...]
        acc[0] = acc_in[...]

    @pl.when(which == 1)
    def _():
        qx[...] = qs_ref[...]
        m_ref[0] = jnp.full(m_in.shape, LOW, F32)
        acc[0] = jnp.zeros(acc_in.shape, F32)

    @pl.loop(0, 3)
    def _(b):
        @pl.when(flags[4 * which + b] == 1)
        def _():
            absorb(qx, kx.at[b], vx.at[b], m_ref.at[0], acc.at[0])


def attend_middle(flags, q, qs, m, acc, kv0, kv1, kv2):
    rows = q.shape[0]
    whole2 = pl.BlockSpec((rows, HD), lambda t, f: (0, 0))
    whole3 = pl.BlockSpec((2, rows, HD), lambda t, f: (0, 0, 0))
    return pl.pallas_call(
        middle_kernel,
        grid_spec=pltpu.PrefetchScalarGridSpec(
            num_scalar_prefetch=1,
            grid=(2,),
            in_specs=[
                whole2,
                whole2,
                whole2,
                pl.BlockSpec((rows, 2 * HD), lambda t, f: (0, 0)),
                whole3,
                whole3,
                whole3,
            ],
            out_specs=[
                pl.BlockSpec((1, rows, HD), lambda t, f: (t, 0, 0)),
                pl.BlockSpec((1, rows, 2 * HD), lambda t, f: (t, 0, 0)),
            ],
            scratch_shapes=[
                pltpu.VMEM((rows, HD), BF),
                pltpu.VMEM((3, HD, rows), BF),
                pltpu.VMEM((3, rows, 2 * HD), BF),
            ],
        ),
        out_shape=[
            jax.ShapeDtypeStruct((2, rows, HD), F32),
            jax.ShapeDtypeStruct((2, rows, 2 * HD), F32),
        ],
        compiler_params=params(40),
        cost_estimate=pl.CostEstimate(flops=8 << 30, bytes_accessed=6 << 20, transcendentals=0),
        name="attend_middle",
    )(flags, q, qs, m, acc, kv0, kv1, kv2)


def last_kernel(flags, q_ref, qs_ref, m_in, acc_in, k3, v3, o_ref, os_ref, lse_ref, qx, kx, vx, m_ref, acc):
    which = pl.program_id(0)
    m_ref[...] = m_in[0]
    acc[...] = acc_in[0]

    @pl.when(which == 0)
    def _():
        load_block(kx, vx, k3[...], v3[...])
        qx[...] = q_ref[...]

    @pl.when(which == 1)
    def _():
        qx[...] = qs_ref[...]

    @pl.when(flags[4 * which + 3] == 1)
    def _():
        absorb(qx, kx, vx, m_ref, acc)

    total = acc[:, HD:]
    o = acc[:, :HD] / total
    lse = m_ref[...] * EXP2_SCALE + jnp.log2(total)
    for i in range(lse.shape[0] // SUB):
        lse_ref[0, i] = lse[i * SUB : (i + 1) * SUB].T[:1]

    @pl.when(which == 0)
    def _():
        o_ref[...] = o

    @pl.when(which == 1)
    def _():
        os_ref[...] = o.astype(BF)


def attend_last(flags, q, qs, m, acc, k3, v3):
    rows = q.shape[0]
    n = rows // SUB
    whole2 = pl.BlockSpec((rows, HD), lambda t, f: (0, 0))
    return pl.pallas_call(
        last_kernel,
        grid_spec=pltpu.PrefetchScalarGridSpec(
            num_scalar_prefetch=1,
            grid=(2,),
            in_specs=[
                whole2,
                whole2,
                pl.BlockSpec((1, rows, HD), lambda t, f: (t, 0, 0)),
                pl.BlockSpec((1, rows, 2 * HD), lambda t, f: (t, 0, 0)),
                whole2,
                whole2,
            ],
            out_specs=[whole2, whole2, pl.BlockSpec((1, n, 1, SUB), lambda t, f: (t, 0, 0, 0))],
            scratch_shapes=[
                pltpu.VMEM((rows, HD), BF),
                pltpu.VMEM((HD, rows), BF),
                pltpu.VMEM((rows, 2 * HD), BF),
                pltpu.VMEM((rows, HD), F32),
                pltpu.VMEM((rows, 2 * HD), F32),
            ],
        ),
        out_shape=[
            jax.ShapeDtypeStruct((rows, HD), F32),
            jax.ShapeDtypeStruct((rows, HD), BF),
            jax.ShapeDtypeStruct((2, n, 1, SUB), F32),
        ],
        compiler_params=params(40),
        cost_estimate=pl.CostEstimate(flops=3 << 30, bytes_accessed=6 << 20, transcendentals=0),
        name="attend_last",
    )(flags, q, qs, m, acc, k3, v3)


def cross_queries(z, parts, weights):
    total = 0.0
    for back, part in parts:
        a = jnp.concatenate([part[h] for h in range(part.shape[0])], axis=1)
        w = lax.dynamic_index_in_dim(weights, (z + 8 - back) % 8, 0, keepdims=False)
        total = total + jnp.dot(a, w, preferred_element_type=F32)
    return total


def project_kernel(info, a_ref, b_ref, w_ref, k_ref, v_ref):
    g = pl.program_id(0)
    slots = a_ref.shape[0]

    def pick(n):
        slot = jnp.maximum(info[2 * g + n], 0)
        at = slot & (slots - 1)
        return jnp.where(slot < slots, a_ref[at], b_ref[at])

    states = jnp.concatenate([pick(0), pick(1)], axis=0)
    both = jnp.dot(states, w_ref[...], preferred_element_type=F32).astype(BF)
    half = both.shape[1] // 2
    k_ref[0] = both[:, :half].T
    v_ref[0] = both[:, half:]


def project(info, held_a, held_b, weights):
    n, length, width = held_a.shape
    groups = info.shape[0] // 2
    half = weights.shape[1] // 2
    whole = pl.BlockSpec((n, length, width), lambda g, s: (0, 0, 0))
    return pl.pallas_call(
        project_kernel,
        grid_spec=pltpu.PrefetchScalarGridSpec(
            num_scalar_prefetch=1,
            grid=(groups,),
            in_specs=[whole, whole, pl.BlockSpec(weights.shape, lambda g, s: (0, 0))],
            out_specs=[
                pl.BlockSpec((1, half, 2 * length), lambda g, s: (g, 0, 0)),
                pl.BlockSpec((1, 2 * length, half), lambda g, s: (g, 0, 0)),
            ],
        ),
        out_shape=[
            jax.ShapeDtypeStruct((groups, half, 2 * length), BF),
            jax.ShapeDtypeStruct((groups, 2 * length, half), BF),
        ],
        compiler_params=params(40),
        cost_estimate=pl.CostEstimate(flops=4 << 30, bytes_accessed=12 << 20, transcendentals=0),
        name="project",
    )(info, held_a, held_b, weights)


def cross_kernel(info, qa_ref, qb_ref, k_ref, v_ref, o_ref, lse_ref):
    step = pl.program_id(0)
    per = k_ref.shape[0]
    group = lse_ref.shape[2]
    late = step * 2 >= pl.num_programs(0)
    for c in range(per):
        rows = slice(c * group, (c + 1) * group)
        g = per * step + c
        q = jnp.where(late, qb_ref[rows], qa_ref[rows])
        first, second = info[2 * g] >= 0, info[2 * g + 1] >= 0
        column = lax.broadcasted_iota(jnp.int32, (1, k_ref.shape[2]), 1)
        bias = jnp.where(
            column < k_ref.shape[2] // 2, jnp.where(first, 0.0, LOW), jnp.where(second, 0.0, LOW)
        )
        some = first | second
        lane = lax.broadcasted_iota(jnp.int32, (group, HD), 1)
        stats = jnp.full((group, HD), LOW, F32)
        for r in range(4):
            cut = slice(r * HD, (r + 1) * HD)
            s = jnp.dot(q[:, cut], k_ref[c, cut, :], preferred_element_type=F32) + bias
            top = jnp.max(s, axis=1, keepdims=True)
            p = jnp.exp2((s - top) * EXP2_SCALE)
            total = jnp.sum(p, axis=1, keepdims=True)
            o = jnp.dot(p.astype(BF), v_ref[c, :, cut], preferred_element_type=F32) / total
            o_ref[r, rows] = o.astype(BF)
            stats = jnp.where((lane == r) & some, top * EXP2_SCALE + jnp.log2(total), stats)
        lse_ref[c] = stats.T[:8]


def cross(info, queries_a, queries_b, keys, values):
    groups = keys.shape[0]
    per = 2
    steps = groups // per
    group = queries_a.shape[0] * 2 // groups
    width = queries_a.shape[1]
    return pl.pallas_call(
        cross_kernel,
        grid_spec=pltpu.PrefetchScalarGridSpec(
            num_scalar_prefetch=1,
            grid=(steps,),
            in_specs=[
                pl.BlockSpec((per * group, width), lambda g, s: (jnp.minimum(g, steps // 2 - 1), 0)),
                pl.BlockSpec((per * group, width), lambda g, s: (jnp.maximum(g - steps // 2, 0), 0)),
                pl.BlockSpec((per,) + keys.shape[1:], lambda g, s: (g, 0, 0)),
                pl.BlockSpec((per,) + values.shape[1:], lambda g, s: (g, 0, 0)),
            ],
            out_specs=[
                pl.BlockSpec((4, per * group, HD), lambda g, s: (0, g, 0)),
                pl.BlockSpec((per, 8, group), lambda g, s: (g, 0, 0)),
            ],
        ),
        out_shape=[
            jax.ShapeDtypeStruct((4, groups * group, HD), BF),
            jax.ShapeDtypeStruct((groups, 8, group), F32),
        ],
        compiler_params=params(32),
        cost_estimate=pl.CostEstimate(flops=1 << 30, bytes_accessed=5 << 20, transcendentals=0),
        name="cross",
    )(info, queries_a, queries_b, keys, values)


def merge(o_a, lse_a, o_b, lse_b):
    top = jnp.maximum(lse_a, lse_b)
    e_a = jnp.exp2(lse_a - top)
    e_b = jnp.exp2(lse_b - top)
    return ((o_a.astype(F32) * e_a + o_b.astype(F32) * e_b) / (e_a + e_b)).astype(BF)


def local(q, k, v, states, nb_shard, nb_row, wk, wv, wq):
    rows = q.shape[0]
    quarter = rows // 4
    y = lax.axis_index("y")
    z = lax.axis_index("z")
    x_lo = lax.axis_index("x_lo")
    core = lax.axis_index("core")
    late = lax.axis_index("x_hi") == 1
    db_index = lax.axis_index(DB)

    kv0, shard, row = lax.optimization_barrier((jnp.stack([k, v]), nb_shard, nb_row))

    place = 2 * lax.broadcasted_iota(jnp.int32, nb_shard.shape, 0) + lax.broadcasted_iota(
        jnp.int32, nb_shard.shape, 1
    )
    coded = place * states.shape[0] + row
    asked = shard == db_index
    none = nb_shard.size * states.shape[0]
    first = jnp.min(jnp.where(asked, coded, none)) & (states.shape[0] - 1)
    last = jnp.max(jnp.where(asked, coded, 0)) & (states.shape[0] - 1)
    pair = jnp.concatenate(
        [lax.dynamic_slice_in_dim(states, i, 1, 0) for i in (first, last)], axis=0
    )
    held_a = lax.all_gather(pair, "z", axis=0, tiled=True)

    kv1 = ring(kv0, "y", 1)
    kv2 = ring(kv0, "y", -1)
    qs = lax.ppermute(q, "x_hi", [(1, 0)])
    k3 = ring(kv1[0], "y", 1)
    v3 = ring(kv2[1], "y", -1)
    flags = jnp.stack([y < 0, y >= 1, y >= 3, y >= 2] + [~late] * 4).astype(jnp.int32)
    m, acc = attend_own(q, kv0)
    m, acc = attend_middle(flags, q, qs, m, acc, kv0, kv1, kv2)
    wall = jnp.concatenate([wq, wk, wv], axis=0)
    half = wall.shape[0] // 2
    w_up = ring(wall[:half], XX, -1)
    w_down = ring(wall[half:], XX, 1)
    o, o_sent, lse = attend_last(flags, q, qs, m, acc, k3, v3)
    lse, lse_sent = lse[0], lse[1]

    o_sent, lse_sent, w_up, w_down = lax.optimization_barrier((o_sent, lse_sent, w_up, w_down))
    o_back = lax.ppermute(o_sent, "x_hi", [(0, 1)])
    lse_back = lax.ppermute(lse_sent, "x_hi", [(0, 1)])
    w_x = jnp.concatenate([w_up, w_down], axis=0)
    w4 = jnp.concatenate([wall, swap(wall, "core"), w_x, swap(w_x, "core")], axis=1)
    depth, width = wq.shape[0], wk.shape[0]
    wq4 = w4[:depth].reshape(8, depth // 8, 4 * HD)
    wkv4 = jnp.concatenate([w4[depth : depth + width], w4[depth + width :]], axis=1)
    o_back, lse_back, wq4, wkv4 = lax.optimization_barrier((o_back, lse_back, wq4, wkv4))

    lse_back = jnp.where(late, lse_back.reshape(rows, 1), LOW)
    self_out = merge(o, lse.reshape(rows, 1), o_back, lse_back)

    held_b = swap(held_a, "core")
    same = nb_shard.reshape(-1)[:, None] == nb_shard.reshape(-1)[None, :]
    n = nb_shard.size
    before = lax.broadcasted_iota(jnp.int32, (n, n), 1) < lax.broadcasted_iota(jnp.int32, (n, n), 0)
    rank = jnp.max((same & before).astype(jnp.int32), axis=1)
    shard = nb_shard.reshape(-1)
    slot = ((shard % 2) ^ core) * 16 + (shard // 4) * 2 + rank
    slot = jnp.where((shard // 2) % 2 == x_lo, slot, -1).reshape(4, n // 4)
    info = jnp.concatenate(
        [
            lax.dynamic_slice_in_dim(slot, 2 * x_lo + core, 1, 0),
            lax.dynamic_slice_in_dim(slot, 2 * (1 - x_lo) + core, 1, 0),
        ],
        axis=1,
    ).reshape(-1)
    keys, values = project(info, held_a, held_b, wkv4)

    mine = lax.all_to_all(self_out.reshape(4, quarter, HD), XC, 0, 0)
    f1 = ring(mine, "z", 1)
    b1 = ring(mine, "z", -1)
    f2 = ring(f1, "z", 1)
    b2 = ring(b1, "z", -1)
    f3 = ring(f2, "z", 1)
    b3 = ring(b2, "z", -1)
    f3, b3, keys, values = lax.optimization_barrier((f3, b3, keys, values))
    far_f = ring(f3[:2], "z", 1)
    far_b = ring(b3[2:], "z", -1)
    near = cross_queries(
        z, ((0, mine), (1, f1), (2, f2), (3, f3), (5, b3), (6, b2), (7, b1)), wq4
    )
    far_f, far_b, near = lax.optimization_barrier((far_f, far_b, near))
    far = jnp.concatenate([far_f, far_b], axis=0)
    queries = (near + cross_queries(z, ((4, far),), wq4)).astype(BF)

    other = swap(queries, "x_lo")
    other = jnp.concatenate([other[:, 2 * HD :], other[:, : 2 * HD]], axis=1)
    o, lse = cross(info, queries, other, keys, values)

    lse = lse[:, :4].transpose(1, 0, 2).reshape(4, 2, 2 * HD)
    o_got = swap(o[2:], "x_lo").reshape(2, 2, quarter, HD)[:, ::-1]
    lse_got = swap(lse[2:], "x_lo")[:, ::-1]
    both = merge(
        o[:2].reshape(2, 2, quarter, HD), lse[:2][..., None], o_got, lse_got[..., None]
    )
    kept, got = both[0], swap(both[1], "core")
    kept, got = (jnp.where(x_lo == 0, a, a[::-1]) for a in (kept, got))
    cross_out = jnp.where(
        core == 0, jnp.stack([kept, got], axis=1), jnp.stack([got, kept], axis=1)
    ).reshape(rows, HD)
    return (self_out, cross_out)


def solution(mesh):
    fine = Mesh(mesh.devices.reshape(2, 4, 8, 2, 2), AXES)
    return jax.shard_map(
        local,
        mesh=fine,
        in_specs=(
            P(CTX, DB),
            P(CTX, DB),
            P(CTX, DB),
            P(DB, None, None),
            P(CTX, None),
            P(CTX, None),
            P(None, DB),
            P(None, DB),
            P(None, DB),
        ),
        out_specs=(P(CTX, DB), P(CTX, DB)),
        check_vma=False,
    )
```

```python
import functools
import math

import jax
import jax.numpy as jnp
from jax import lax
from jax.experimental import pallas as pl
from jax.experimental.pallas import tpu as pltpu
from jax.sharding import Mesh
from jax.sharding import PartitionSpec as P

HD = 128
AXES = ("x_hi", "y", "z", "x_lo", "core")
CTX = ("x_hi", "y")
DB = ("z", "x_lo", "core")
XC = ("x_lo", "core")
XX = ("x_hi", "x_lo")
LOW = -1e30
EXP2_SCALE = math.log2(math.e) / math.sqrt(HD)
BF = jnp.bfloat16
F32 = jnp.float32


def ring(value, axis, step):
    n = lax.axis_size(axis)
    return lax.ppermute(value, axis, [(i, (i + step) % n) for i in range(n)])


def swap(value, axis):
    return lax.ppermute(value, axis, [(0, 1), (1, 0)])


def params(megabytes):
    return pltpu.CompilerParams(
        dimension_semantics=("arbitrary",), vmem_limit_bytes=megabytes << 20
    )


def dot_t(a, b):
    return lax.dot_general(a, b, (((1,), (1,)), ((), ())), preferred_element_type=F32)


SUB = 256


def load_block(kx, vx, key, value):
    kx[...] = key.T
    vx[:, :HD] = value
    vx[:, HD:] = jnp.ones_like(value)


def absorb(q_ref, kx, vx, m_ref, acc):
    def scores(i):
        return jnp.dot(q_ref[i * SUB : (i + 1) * SUB, :], kx[...], preferred_element_type=F32)

    n = q_ref.shape[0] // SUB
    s = scores(0)
    for i in range(n):
        ahead = scores(i + 1) if i + 1 < n else None
        r = slice(i * SUB, (i + 1) * SUB)
        before = m_ref[r]
        now = jnp.maximum(before, jnp.max(s, axis=1, keepdims=True))
        p = jnp.exp2((s - now[:, :1]) * EXP2_SCALE)
        factor = jnp.exp2((before - now) * EXP2_SCALE)
        m_ref[r] = now
        acc[r] = acc[r] * jnp.concatenate([factor, factor], axis=1) + jnp.dot(
            p.astype(BF), vx[...], preferred_element_type=F32
        )
        s = ahead


def own_kernel(q_ref, kv_ref, m_ref, acc, kx, vx):
    load_block(kx, vx, kv_ref[0], kv_ref[1])

    def scores(i):
        seen = (i + 1) * SUB
        s = jnp.dot(q_ref[i * SUB : seen, :], kx[:, :seen], preferred_element_type=F32)
        row = lax.broadcasted_iota(jnp.int32, s.shape, 0) + i * SUB
        return jnp.where(row >= lax.broadcasted_iota(jnp.int32, s.shape, 1), s, LOW)

    n = q_ref.shape[0] // SUB
    s = scores(0)
    for i in range(n):
        ahead = scores(i + 1) if i + 1 < n else None
        r = slice(i * SUB, (i + 1) * SUB)
        now = jnp.max(s, axis=1, keepdims=True)
        p = jnp.exp2((s - now) * EXP2_SCALE)
        m_ref[r] = jnp.broadcast_to(now, (SUB, HD))
        acc[r] = jnp.dot(p.astype(BF), vx[: (i + 1) * SUB, :], preferred_element_type=F32)
        s = ahead


def attend_own(q, kv):
    rows = q.shape[0]
    return pl.pallas_call(
        own_kernel,
        in_specs=[pl.BlockSpec(memory_space=pltpu.VMEM)] * 2,
        out_specs=[pl.BlockSpec(memory_space=pltpu.VMEM)] * 2,
        out_shape=[jax.ShapeDtypeStruct((rows, HD), F32), jax.ShapeDtypeStruct((rows, 2 * HD), F32)],
        scratch_shapes=[pltpu.VMEM((HD, rows), BF), pltpu.VMEM((rows, 2 * HD), BF)],
        compiler_params=pltpu.CompilerParams(vmem_limit_bytes=24 << 20),
        cost_estimate=pl.CostEstimate(flops=1 << 30, bytes_accessed=3 << 20, transcendentals=0),
        name="attend_own",
    )(q, kv)


def middle_kernel(flags, q_ref, qs_ref, m_in, acc_in, kv0, kv1, kv2, m_ref, acc, qx, kx, vx):
    which = pl.program_id(0)

    @pl.when(which == 0)
    def _():
        for b, kv in enumerate((kv0, kv1, kv2)):
            load_block(kx.at[b], vx.at[b], kv[0], kv[1])
        qx[...] = q_ref[...]
        m_ref[0] = m_in[...]
        acc[0] = acc_in[...]

    @pl.when(which == 1)
    def _():
        qx[...] = qs_ref[...]
        m_ref[0] = jnp.full(m_in.shape, LOW, F32)
        acc[0] = jnp.zeros(acc_in.shape, F32)

    @pl.loop(0, 3)
    def _(b):
        @pl.when(flags[4 * which + b] == 1)
        def _():
            absorb(qx, kx.at[b], vx.at[b], m_ref.at[0], acc.at[0])


def attend_middle(flags, q, qs, m, acc, kv0, kv1, kv2):
    rows = q.shape[0]
    whole2 = pl.BlockSpec((rows, HD), lambda t, f: (0, 0))
    whole3 = pl.BlockSpec((2, rows, HD), lambda t, f: (0, 0, 0))
    return pl.pallas_call(
        middle_kernel,
        grid_spec=pltpu.PrefetchScalarGridSpec(
            num_scalar_prefetch=1,
            grid=(2,),
            in_specs=[
                whole2,
                whole2,
                whole2,
                pl.BlockSpec((rows, 2 * HD), lambda t, f: (0, 0)),
                whole3,
                whole3,
                whole3,
            ],
            out_specs=[
                pl.BlockSpec((1, rows, HD), lambda t, f: (t, 0, 0)),
                pl.BlockSpec((1, rows, 2 * HD), lambda t, f: (t, 0, 0)),
            ],
            scratch_shapes=[
                pltpu.VMEM((rows, HD), BF),
                pltpu.VMEM((3, HD, rows), BF),
                pltpu.VMEM((3, rows, 2 * HD), BF),
            ],
        ),
        out_shape=[
            jax.ShapeDtypeStruct((2, rows, HD), F32),
            jax.ShapeDtypeStruct((2, rows, 2 * HD), F32),
        ],
        compiler_params=params(40),
        cost_estimate=pl.CostEstimate(flops=8 << 30, bytes_accessed=6 << 20, transcendentals=0),
        name="attend_middle",
    )(flags, q, qs, m, acc, kv0, kv1, kv2)


def last_kernel(flags, q_ref, qs_ref, m_in, acc_in, k3, v3, o_ref, os_ref, lse_ref, qx, kx, vx, m_ref, acc):
    which = pl.program_id(0)
    m_ref[...] = m_in[0]
    acc[...] = acc_in[0]

    @pl.when(which == 0)
    def _():
        load_block(kx, vx, k3[...], v3[...])
        qx[...] = q_ref[...]

    @pl.when(which == 1)
    def _():
        qx[...] = qs_ref[...]

    @pl.when(flags[4 * which + 3] == 1)
    def _():
        absorb(qx, kx, vx, m_ref, acc)

    total = acc[:, HD:]
    o = acc[:, :HD] / total
    lse = m_ref[...] * EXP2_SCALE + jnp.log2(total)
    for i in range(lse.shape[0] // SUB):
        lse_ref[0, i] = lse[i * SUB : (i + 1) * SUB].T[:1]

    @pl.when(which == 0)
    def _():
        o_ref[...] = o

    @pl.when(which == 1)
    def _():
        os_ref[...] = o.astype(BF)


def attend_last(flags, q, qs, m, acc, k3, v3):
    rows = q.shape[0]
    n = rows // SUB
    whole2 = pl.BlockSpec((rows, HD), lambda t, f: (0, 0))
    return pl.pallas_call(
        last_kernel,
        grid_spec=pltpu.PrefetchScalarGridSpec(
            num_scalar_prefetch=1,
            grid=(2,),
            in_specs=[
                whole2,
                whole2,
                pl.BlockSpec((1, rows, HD), lambda t, f: (t, 0, 0)),
                pl.BlockSpec((1, rows, 2 * HD), lambda t, f: (t, 0, 0)),
                whole2,
                whole2,
            ],
            out_specs=[whole2, whole2, pl.BlockSpec((1, n, 1, SUB), lambda t, f: (t, 0, 0, 0))],
            scratch_shapes=[
                pltpu.VMEM((rows, HD), BF),
                pltpu.VMEM((HD, rows), BF),
                pltpu.VMEM((rows, 2 * HD), BF),
                pltpu.VMEM((rows, HD), F32),
                pltpu.VMEM((rows, 2 * HD), F32),
            ],
        ),
        out_shape=[
            jax.ShapeDtypeStruct((rows, HD), F32),
            jax.ShapeDtypeStruct((rows, HD), BF),
            jax.ShapeDtypeStruct((2, n, 1, SUB), F32),
        ],
        compiler_params=params(40),
        cost_estimate=pl.CostEstimate(flops=3 << 30, bytes_accessed=6 << 20, transcendentals=0),
        name="attend_last",
    )(flags, q, qs, m, acc, k3, v3)


def cross_queries(z, parts, weights):
    total = 0.0
    for back, part in parts:
        a = jnp.concatenate([part[h] for h in range(part.shape[0])], axis=1)
        w = lax.dynamic_index_in_dim(weights, (z + 8 - back) % 8, 0, keepdims=False)
        total = total + jnp.dot(a, w, preferred_element_type=F32)
    return total


def project_kernel(info, a_ref, b_ref, w0, w1, w2, w3, k_ref, v_ref, w_ref):
    g = pl.program_id(0)
    slots = a_ref.shape[0]
    width = a_ref.shape[2]

    @pl.when(g == 0)
    def _():
        for r, piece in enumerate((w0, w1, w2, w3)):
            w_ref[:, r * HD : (r + 1) * HD] = piece[:width]
            w_ref[:, (4 + r) * HD : (5 + r) * HD] = piece[width:]

    def pick(n):
        slot = jnp.maximum(info[2 * g + n], 0)
        at = slot & (slots - 1)
        return jnp.where(slot < slots, a_ref[at], b_ref[at])

    states = jnp.concatenate([pick(0), pick(1)], axis=0)
    both = jnp.dot(states, w_ref[...], preferred_element_type=F32).astype(BF)
    half = both.shape[1] // 2
    k_ref[0] = both[:, :half].T
    v_ref[0] = both[:, half:]


def project(info, held_a, held_b, pieces):
    n, length, width = held_a.shape
    groups = info.shape[0] // 2
    half = 4 * HD
    whole = pl.BlockSpec((n, length, width), lambda g, s: (0, 0, 0))
    return pl.pallas_call(
        project_kernel,
        grid_spec=pltpu.PrefetchScalarGridSpec(
            num_scalar_prefetch=1,
            grid=(groups,),
            in_specs=[whole, whole] + [pl.BlockSpec((2 * width, HD), lambda g, s: (0, 0))] * 4,
            out_specs=[
                pl.BlockSpec((1, half, 2 * length), lambda g, s: (g, 0, 0)),
                pl.BlockSpec((1, 2 * length, half), lambda g, s: (g, 0, 0)),
            ],
            scratch_shapes=[pltpu.VMEM((width, 2 * half), BF)],
        ),
        out_shape=[
            jax.ShapeDtypeStruct((groups, half, 2 * length), BF),
            jax.ShapeDtypeStruct((groups, 2 * length, half), BF),
        ],
        compiler_params=params(40),
        cost_estimate=pl.CostEstimate(flops=4 << 30, bytes_accessed=12 << 20, transcendentals=0),
        name="project",
    )(info, held_a, held_b, *pieces)


def cross_kernel(info, q_ref, k_ref, v_ref, o_ref, lse_ref):
    step = pl.program_id(0)
    per = k_ref.shape[0]
    group = lse_ref.shape[2]
    for c in range(per):
        rows = slice(c * group, (c + 1) * group)
        g = per * step + c
        q = q_ref[rows]
        first, second = info[2 * g] >= 0, info[2 * g + 1] >= 0
        column = lax.broadcasted_iota(jnp.int32, (1, k_ref.shape[2]), 1)
        bias = jnp.where(
            column < k_ref.shape[2] // 2, jnp.where(first, 0.0, LOW), jnp.where(second, 0.0, LOW)
        )
        some = first | second
        lane = lax.broadcasted_iota(jnp.int32, (group, HD), 1)
        stats = jnp.full((group, HD), LOW, F32)
        for r in range(4):
            cut = slice(r * HD, (r + 1) * HD)
            s = jnp.dot(q[:, cut], k_ref[c, cut, :], preferred_element_type=F32) + bias
            top = jnp.max(s, axis=1, keepdims=True)
            p = jnp.exp2((s - top) * EXP2_SCALE)
            total = jnp.sum(p, axis=1, keepdims=True)
            o = jnp.dot(p.astype(BF), v_ref[c, :, cut], preferred_element_type=F32) / total
            o_ref[r, rows] = o.astype(BF)
            stats = jnp.where((lane == r) & some, top * EXP2_SCALE + jnp.log2(total), stats)
        lse_ref[c] = stats.T[:8]


def cross(half, info, queries, keys, values):
    groups = keys.shape[0] // 2
    per = 2
    start = half * groups // per
    group = queries.shape[0] // groups
    width = queries.shape[1]
    return pl.pallas_call(
        cross_kernel,
        grid_spec=pltpu.PrefetchScalarGridSpec(
            num_scalar_prefetch=1,
            grid=(groups // per,),
            in_specs=[
                pl.BlockSpec((per * group, width), lambda g, s: (g, 0)),
                pl.BlockSpec((per,) + keys.shape[1:], lambda g, s: (start + g, 0, 0)),
                pl.BlockSpec((per,) + values.shape[1:], lambda g, s: (start + g, 0, 0)),
            ],
            out_specs=[
                pl.BlockSpec((4, per * group, HD), lambda g, s: (0, g, 0)),
                pl.BlockSpec((per, 8, group), lambda g, s: (g, 0, 0)),
            ],
        ),
        out_shape=[
            jax.ShapeDtypeStruct((4, groups * group, HD), BF),
            jax.ShapeDtypeStruct((groups, 8, group), F32),
        ],
        compiler_params=params(24),
        cost_estimate=pl.CostEstimate(flops=2 << 30, bytes_accessed=3 << 20, transcendentals=0),
        name="cross",
    )(info, queries, keys, values)


def merge(o_a, lse_a, o_b, lse_b):
    top = jnp.maximum(lse_a, lse_b)
    e_a = jnp.exp2(lse_a - top)
    e_b = jnp.exp2(lse_b - top)
    return ((o_a.astype(F32) * e_a + o_b.astype(F32) * e_b) / (e_a + e_b)).astype(BF)


def local(q, k, v, states, nb_shard, nb_row, wk, wv, wq):
    rows = q.shape[0]
    quarter = rows // 4
    y = lax.axis_index("y")
    z = lax.axis_index("z")
    x_lo = lax.axis_index("x_lo")
    core = lax.axis_index("core")
    late = lax.axis_index("x_hi") == 1
    db_index = lax.axis_index(DB)

    kv0, shard, row = lax.optimization_barrier((jnp.stack([k, v]), nb_shard, nb_row))

    place = 2 * lax.broadcasted_iota(jnp.int32, nb_shard.shape, 0) + lax.broadcasted_iota(
        jnp.int32, nb_shard.shape, 1
    )
    coded = place * states.shape[0] + row
    asked = shard == db_index
    none = nb_shard.size * states.shape[0]
    first = jnp.min(jnp.where(asked, coded, none)) & (states.shape[0] - 1)
    last = jnp.max(jnp.where(asked, coded, 0)) & (states.shape[0] - 1)
    pair = jnp.concatenate(
        [lax.dynamic_slice_in_dim(states, i, 1, 0) for i in (first, last)], axis=0
    )
    held_a = lax.all_gather(pair, "z", axis=0, tiled=True)

    kv1 = ring(kv0, "y", 1)
    kv2 = ring(kv0, "y", -1)
    qs = lax.ppermute(q, "x_hi", [(1, 0)])
    k3 = ring(kv1[0], "y", 1)
    v3 = ring(kv2[1], "y", -1)
    flags = jnp.stack([y < 0, y >= 1, y >= 3, y >= 2] + [~late] * 4).astype(jnp.int32)
    m, acc = attend_own(q, kv0)
    m, acc = attend_middle(flags, q, qs, m, acc, kv0, kv1, kv2)
    skip = 2 * wk.shape[0]
    cut = (wq.shape[0] - skip) // 2
    up, down = jnp.concatenate([wk, wv, wq[:cut]], axis=0), wq[cut:]
    up_x = ring(up, XX, -1)
    down_x = ring(down, XX, 1)
    o, o_sent, lse = attend_last(flags, q, qs, m, acc, k3, v3)
    lse, lse_sent = lse[0], lse[1]

    o_back = lax.ppermute(o_sent, "x_hi", [(0, 1)])
    lse_back = lax.ppermute(lse_sent, "x_hi", [(0, 1)])
    o_back, lse_back, up_x, down_x = lax.optimization_barrier((o_back, lse_back, up_x, down_x))
    ups = (up, swap(up, "core"), up_x, swap(up_x, "core"))
    downs = (down, swap(down, "core"), down_x, swap(down_x, "core"))
    wq4 = jnp.concatenate(
        [
            jnp.concatenate([a[skip:] for a in ups], axis=1),
            jnp.concatenate(downs, axis=1),
        ],
        axis=0,
    ).reshape(8, -1, 4 * HD)

    lse_back = jnp.where(late, lse_back.reshape(rows, 1), LOW)
    self_out = merge(o, lse.reshape(rows, 1), o_back, lse_back)

    same = nb_shard.reshape(-1)[:, None] == nb_shard.reshape(-1)[None, :]
    n = nb_shard.size
    before = lax.broadcasted_iota(jnp.int32, (n, n), 1) < lax.broadcasted_iota(jnp.int32, (n, n), 0)
    rank = jnp.max((same & before).astype(jnp.int32), axis=1)
    shard = nb_shard.reshape(-1)
    slot = ((shard % 2) ^ core) * 16 + (shard // 4) * 2 + rank
    slot = jnp.where((shard // 2) % 2 == x_lo, slot, -1).reshape(4, n // 4)
    info = jnp.concatenate(
        [
            lax.dynamic_slice_in_dim(slot, 2 * x_lo + core, 1, 0),
            lax.dynamic_slice_in_dim(slot, 2 * (1 - x_lo) + core, 1, 0),
        ],
        axis=1,
    ).reshape(-1)

    mine = lax.all_to_all(self_out.reshape(4, quarter, HD), XC, 0, 0)
    f1 = ring(mine, "z", 1)
    b1 = ring(mine, "z", -1)
    f1, b1, held_a, wq4 = lax.optimization_barrier((f1, b1, held_a, wq4))
    held_b = swap(held_a, "core")
    f2 = ring(f1, "z", 1)
    b2 = ring(b1, "z", -1)
    f3 = ring(f2, "z", 1)
    b3 = ring(b2, "z", -1)
    keys, values = project(info, held_a, held_b, ups)
    f3, b3, keys, values = lax.optimization_barrier((f3, b3, keys, values))
    far_f = ring(f3[:2], "z", 1)
    far_b = ring(b3[2:], "z", -1)
    near = cross_queries(
        z, ((0, mine), (1, f1), (2, f2), (3, f3), (5, b3), (6, b2), (7, b1)), wq4
    )
    far_f, far_b, near = lax.optimization_barrier((far_f, far_b, near))
    far = jnp.concatenate([far_f, far_b], axis=0)
    queries = (near + cross_queries(z, ((4, far),), wq4)).astype(BF)

    other = swap(queries, "x_lo")
    o_a, lse_a = cross(0, info[: n // 4], queries, keys, values)
    got_a = swap(o_a[2:], "x_lo")
    other = jnp.concatenate([other[:, 2 * HD :], other[:, : 2 * HD]], axis=1)
    o_b, lse_b = cross(1, info[n // 4 :], other, keys, values)
    got_b = swap(o_b[2:], "x_lo")

    lse = jnp.stack([lse_a[:, :4], lse_b[:, :4]]).transpose(2, 0, 1, 3).reshape(4, 2, quarter, 1)
    lse_got = swap(lse[2:].reshape(2, 2, quarter), "x_lo")[..., None]
    both = jnp.stack(
        [
            merge(o_a[:2], lse[:2, 0], got_b, lse_got[:, 1]),
            merge(o_b[:2], lse[:2, 1], got_a, lse_got[:, 0]),
        ],
        axis=1,
    )
    kept, got = both[0], swap(both[1], "core")
    kept, got = (jnp.where(x_lo == 0, a, a[::-1]) for a in (kept, got))
    cross_out = jnp.where(
        core == 0, jnp.stack([kept, got], axis=1), jnp.stack([got, kept], axis=1)
    ).reshape(rows, HD)
    return (self_out, cross_out)


def solution(mesh):
    fine = Mesh(mesh.devices.reshape(2, 4, 8, 2, 2), AXES)
    return jax.shard_map(
        local,
        mesh=fine,
        in_specs=(
            P(CTX, DB),
            P(CTX, DB),
            P(CTX, DB),
            P(DB, None, None),
            P(CTX, None),
            P(CTX, None),
            P(None, DB),
            P(None, DB),
            P(None, DB),
        ),
        out_specs=(P(CTX, DB), P(CTX, DB)),
        check_vma=False,
    )
```

```python
import functools
import math

import jax
import jax.numpy as jnp
from jax import lax
from jax.experimental import pallas as pl
from jax.experimental.pallas import tpu as pltpu
from jax.sharding import Mesh
from jax.sharding import PartitionSpec as P

HD = 128
AXES = ("x_hi", "y", "z", "x_lo", "core")
CTX = ("x_hi", "y")
DB = ("z", "x_lo", "core")
XC = ("x_lo", "core")
XX = ("x_hi", "x_lo")
LOW = -1e30
EXP2_SCALE = math.log2(math.e) / math.sqrt(HD)
BF = jnp.bfloat16
F32 = jnp.float32


def ring(value, axis, step):
    n = lax.axis_size(axis)
    return lax.ppermute(value, axis, [(i, (i + step) % n) for i in range(n)])


def swap(value, axis):
    return lax.ppermute(value, axis, [(0, 1), (1, 0)])


def params(megabytes):
    return pltpu.CompilerParams(
        dimension_semantics=("arbitrary",), vmem_limit_bytes=megabytes << 20
    )


def dot_t(a, b):
    return lax.dot_general(a, b, (((1,), (1,)), ((), ())), preferred_element_type=F32)


SUB = 256


def load_block(kx, vx, key, value):
    kx[...] = key.T
    vx[:, :HD] = value
    vx[:, HD:] = jnp.ones_like(value)


def absorb(q_ref, kx, vx, m_ref, acc):
    def scores(i):
        return jnp.dot(q_ref[i * SUB : (i + 1) * SUB, :], kx[...], preferred_element_type=F32)

    n = q_ref.shape[0] // SUB
    s = scores(0)
    for i in range(n):
        ahead = scores(i + 1) if i + 1 < n else None
        r = slice(i * SUB, (i + 1) * SUB)
        before = m_ref[r]
        now = jnp.maximum(before, jnp.max(s, axis=1, keepdims=True))
        p = jnp.exp2((s - now[:, :1]) * EXP2_SCALE)
        factor = jnp.exp2((before - now) * EXP2_SCALE)
        m_ref[r] = now
        acc[r] = acc[r] * jnp.concatenate([factor, factor], axis=1) + jnp.dot(
            p.astype(BF), vx[...], preferred_element_type=F32
        )
        s = ahead


def own_kernel(q_ref, kv_ref, m_ref, acc, kx, vx):
    load_block(kx, vx, kv_ref[0], kv_ref[1])

    def scores(i):
        seen = (i + 1) * SUB
        s = jnp.dot(q_ref[i * SUB : seen, :], kx[:, :seen], preferred_element_type=F32)
        row = lax.broadcasted_iota(jnp.int32, s.shape, 0) + i * SUB
        return jnp.where(row >= lax.broadcasted_iota(jnp.int32, s.shape, 1), s, LOW)

    n = q_ref.shape[0] // SUB
    s = scores(0)
    for i in range(n):
        ahead = scores(i + 1) if i + 1 < n else None
        r = slice(i * SUB, (i + 1) * SUB)
        now = jnp.max(s, axis=1, keepdims=True)
        p = jnp.exp2((s - now) * EXP2_SCALE)
        m_ref[r] = jnp.broadcast_to(now, (SUB, HD))
        acc[r] = jnp.dot(p.astype(BF), vx[: (i + 1) * SUB, :], preferred_element_type=F32)
        s = ahead


def attend_own(q, kv):
    rows = q.shape[0]
    return pl.pallas_call(
        own_kernel,
        in_specs=[pl.BlockSpec(memory_space=pltpu.VMEM)] * 2,
        out_specs=[pl.BlockSpec(memory_space=pltpu.VMEM)] * 2,
        out_shape=[jax.ShapeDtypeStruct((rows, HD), F32), jax.ShapeDtypeStruct((rows, 2 * HD), F32)],
        scratch_shapes=[pltpu.VMEM((HD, rows), BF), pltpu.VMEM((rows, 2 * HD), BF)],
        compiler_params=pltpu.CompilerParams(vmem_limit_bytes=24 << 20),
        cost_estimate=pl.CostEstimate(flops=1 << 30, bytes_accessed=3 << 20, transcendentals=0),
        name="attend_own",
    )(q, kv)


def middle_kernel(flags, q_ref, qs_ref, m_in, acc_in, kv0, kv1, kv2, m_ref, acc, qx, kx, vx):
    which = pl.program_id(0)

    @pl.when(which == 0)
    def _():
        for b, kv in enumerate((kv0, kv1, kv2)):
            load_block(kx.at[b], vx.at[b], kv[0], kv[1])
        qx[...] = q_ref[...]
        m_ref[0] = m_in[...]
        acc[0] = acc_in[...]

    @pl.when(which == 1)
    def _():
        qx[...] = qs_ref[...]
        m_ref[0] = jnp.full(m_in.shape, LOW, F32)
        acc[0] = jnp.zeros(acc_in.shape, F32)

    @pl.loop(0, 3)
    def _(b):
        @pl.when(flags[4 * which + b] == 1)
        def _():
            absorb(qx, kx.at[b], vx.at[b], m_ref.at[0], acc.at[0])


def attend_middle(flags, q, qs, m, acc, kv0, kv1, kv2):
    rows = q.shape[0]
    whole2 = pl.BlockSpec((rows, HD), lambda t, f: (0, 0))
    whole3 = pl.BlockSpec((2, rows, HD), lambda t, f: (0, 0, 0))
    return pl.pallas_call(
        middle_kernel,
        grid_spec=pltpu.PrefetchScalarGridSpec(
            num_scalar_prefetch=1,
            grid=(2,),
            in_specs=[
                whole2,
                whole2,
                whole2,
                pl.BlockSpec((rows, 2 * HD), lambda t, f: (0, 0)),
                whole3,
                whole3,
                whole3,
            ],
            out_specs=[
                pl.BlockSpec((1, rows, HD), lambda t, f: (t, 0, 0)),
                pl.BlockSpec((1, rows, 2 * HD), lambda t, f: (t, 0, 0)),
            ],
            scratch_shapes=[
                pltpu.VMEM((rows, HD), BF),
                pltpu.VMEM((3, HD, rows), BF),
                pltpu.VMEM((3, rows, 2 * HD), BF),
            ],
        ),
        out_shape=[
            jax.ShapeDtypeStruct((2, rows, HD), F32),
            jax.ShapeDtypeStruct((2, rows, 2 * HD), F32),
        ],
        compiler_params=params(40),
        cost_estimate=pl.CostEstimate(flops=8 << 30, bytes_accessed=6 << 20, transcendentals=0),
        name="attend_middle",
    )(flags, q, qs, m, acc, kv0, kv1, kv2)


def last_kernel(flags, q_ref, qs_ref, m_in, acc_in, k3, v3, o_ref, os_ref, lse_ref, qx, kx, vx, m_ref, acc):
    which = pl.program_id(0)
    m_ref[...] = m_in[0]
    acc[...] = acc_in[0]

    @pl.when(which == 0)
    def _():
        load_block(kx, vx, k3[...], v3[...])
        qx[...] = q_ref[...]

    @pl.when(which == 1)
    def _():
        qx[...] = qs_ref[...]

    @pl.when(flags[4 * which + 3] == 1)
    def _():
        absorb(qx, kx, vx, m_ref, acc)

    total = acc[:, HD:]
    o = acc[:, :HD] / total
    lse = m_ref[...] * EXP2_SCALE + jnp.log2(total)
    for i in range(lse.shape[0] // SUB):
        lse_ref[0, i] = lse[i * SUB : (i + 1) * SUB].T[:1]

    @pl.when(which == 0)
    def _():
        o_ref[...] = o

    @pl.when(which == 1)
    def _():
        os_ref[...] = o.astype(BF)


def attend_last(flags, q, qs, m, acc, k3, v3):
    rows = q.shape[0]
    n = rows // SUB
    whole2 = pl.BlockSpec((rows, HD), lambda t, f: (0, 0))
    return pl.pallas_call(
        last_kernel,
        grid_spec=pltpu.PrefetchScalarGridSpec(
            num_scalar_prefetch=1,
            grid=(2,),
            in_specs=[
                whole2,
                whole2,
                pl.BlockSpec((1, rows, HD), lambda t, f: (t, 0, 0)),
                pl.BlockSpec((1, rows, 2 * HD), lambda t, f: (t, 0, 0)),
                whole2,
                whole2,
            ],
            out_specs=[whole2, whole2, pl.BlockSpec((1, n, 1, SUB), lambda t, f: (t, 0, 0, 0))],
            scratch_shapes=[
                pltpu.VMEM((rows, HD), BF),
                pltpu.VMEM((HD, rows), BF),
                pltpu.VMEM((rows, 2 * HD), BF),
                pltpu.VMEM((rows, HD), F32),
                pltpu.VMEM((rows, 2 * HD), F32),
            ],
        ),
        out_shape=[
            jax.ShapeDtypeStruct((rows, HD), F32),
            jax.ShapeDtypeStruct((rows, HD), BF),
            jax.ShapeDtypeStruct((2, n, 1, SUB), F32),
        ],
        compiler_params=params(40),
        cost_estimate=pl.CostEstimate(flops=3 << 30, bytes_accessed=6 << 20, transcendentals=0),
        name="attend_last",
    )(flags, q, qs, m, acc, k3, v3)


def side_kernel(skip, u0, u1, u2, u3, d0, d1, d2, d3, out):
    cut = u0.shape[0] - skip
    for r, (u, d) in enumerate(((u0, d0), (u1, d1), (u2, d2), (u3, d3))):
        out[:cut, r * HD : (r + 1) * HD] = u[skip:]
        out[cut:, r * HD : (r + 1) * HD] = d[...]


def side_by_side(skip, ups, downs):
    depth = ups[0].shape[0] - skip + downs[0].shape[0]
    return pl.pallas_call(
        functools.partial(side_kernel, skip),
        in_specs=[pl.BlockSpec(memory_space=pltpu.VMEM)] * 8,
        out_specs=pl.BlockSpec(memory_space=pltpu.VMEM),
        out_shape=jax.ShapeDtypeStruct((depth, 4 * HD), BF),
        compiler_params=pltpu.CompilerParams(vmem_limit_bytes=24 << 20),
        cost_estimate=pl.CostEstimate(flops=1 << 20, bytes_accessed=10 << 20, transcendentals=0),
        name="side_by_side",
    )(*ups, *downs)


def cross_queries(z, parts, weights):
    total = 0.0
    for back, part in parts:
        a = jnp.concatenate([part[h] for h in range(part.shape[0])], axis=1)
        w = lax.dynamic_index_in_dim(weights, (z + 8 - back) % 8, 0, keepdims=False)
        total = total + jnp.dot(a, w, preferred_element_type=F32)
    return total


def project_kernel(info, a_ref, b_ref, w0, w1, w2, w3, k_ref, v_ref, w_ref):
    g = pl.program_id(0)
    slots = a_ref.shape[0]
    width = a_ref.shape[2]

    @pl.when(g == 0)
    def _():
        for r, piece in enumerate((w0, w1, w2, w3)):
            w_ref[:, r * HD : (r + 1) * HD] = piece[:width]
            w_ref[:, (4 + r) * HD : (5 + r) * HD] = piece[width:]

    def pick(n):
        slot = jnp.maximum(info[4 * g + n], 0)
        at = slot & (slots - 1)
        return jnp.where(slot < slots, a_ref[at], b_ref[at])

    states = jnp.concatenate([pick(n) for n in range(4)], axis=0)
    both = jnp.dot(states, w_ref[...], preferred_element_type=F32).astype(BF)
    half = both.shape[1] // 2
    for c in range(2):
        rows = slice(c * both.shape[0] // 2, (c + 1) * both.shape[0] // 2)
        k_ref[c] = both[rows, :half].T
        v_ref[c] = both[rows, half:]


def project(info, held_a, held_b, pieces):
    n, length, width = held_a.shape
    groups = info.shape[0] // 2
    half = 4 * HD
    whole = pl.BlockSpec((n, length, width), lambda g, s: (0, 0, 0))
    return pl.pallas_call(
        project_kernel,
        grid_spec=pltpu.PrefetchScalarGridSpec(
            num_scalar_prefetch=1,
            grid=(groups // 2,),
            in_specs=[whole, whole] + [pl.BlockSpec((2 * width, HD), lambda g, s: (0, 0))] * 4,
            out_specs=[
                pl.BlockSpec((2, half, 2 * length), lambda g, s: (g, 0, 0)),
                pl.BlockSpec((2, 2 * length, half), lambda g, s: (g, 0, 0)),
            ],
            scratch_shapes=[pltpu.VMEM((width, 2 * half), BF)],
        ),
        out_shape=[
            jax.ShapeDtypeStruct((groups, half, 2 * length), BF),
            jax.ShapeDtypeStruct((groups, 2 * length, half), BF),
        ],
        compiler_params=params(40),
        cost_estimate=pl.CostEstimate(flops=4 << 30, bytes_accessed=12 << 20, transcendentals=0),
        name="project",
    )(info, held_a, held_b, *pieces)


def cross_kernel(info, q_ref, k_ref, v_ref, o_ref, lse_ref):
    step = pl.program_id(0)
    per = k_ref.shape[0]
    group = lse_ref.shape[2]
    for c in range(per):
        rows = slice(c * group, (c + 1) * group)
        g = per * step + c
        q = q_ref[rows]
        first, second = info[2 * g] >= 0, info[2 * g + 1] >= 0
        column = lax.broadcasted_iota(jnp.int32, (1, k_ref.shape[2]), 1)
        bias = jnp.where(
            column < k_ref.shape[2] // 2, jnp.where(first, 0.0, LOW), jnp.where(second, 0.0, LOW)
        )
        some = first | second
        lane = lax.broadcasted_iota(jnp.int32, (group, HD), 1)
        stats = jnp.full((group, HD), LOW, F32)
        for r in range(4):
            cut = slice(r * HD, (r + 1) * HD)
            s = jnp.dot(q[:, cut], k_ref[c, cut, :], preferred_element_type=F32) + bias
            top = jnp.max(s, axis=1, keepdims=True)
            p = jnp.exp2((s - top) * EXP2_SCALE)
            total = jnp.sum(p, axis=1, keepdims=True)
            o = jnp.dot(p.astype(BF), v_ref[c, :, cut], preferred_element_type=F32) / total
            o_ref[r, rows] = o.astype(BF)
            stats = jnp.where((lane == r) & some, top * EXP2_SCALE + jnp.log2(total), stats)
        lse_ref[c] = stats.T[:8]


def cross(half, info, queries, keys, values):
    groups = keys.shape[0] // 2
    per = 2
    start = half * groups // per
    group = queries.shape[0] // groups
    width = queries.shape[1]
    return pl.pallas_call(
        cross_kernel,
        grid_spec=pltpu.PrefetchScalarGridSpec(
            num_scalar_prefetch=1,
            grid=(groups // per,),
            in_specs=[
                pl.BlockSpec((per * group, width), lambda g, s: (g, 0)),
                pl.BlockSpec((per,) + keys.shape[1:], lambda g, s: (start + g, 0, 0)),
                pl.BlockSpec((per,) + values.shape[1:], lambda g, s: (start + g, 0, 0)),
            ],
            out_specs=[
                pl.BlockSpec((4, per * group, HD), lambda g, s: (0, g, 0)),
                pl.BlockSpec((per, 8, group), lambda g, s: (g, 0, 0)),
            ],
        ),
        out_shape=[
            jax.ShapeDtypeStruct((4, groups * group, HD), BF),
            jax.ShapeDtypeStruct((groups, 8, group), F32),
        ],
        compiler_params=params(24),
        cost_estimate=pl.CostEstimate(flops=2 << 30, bytes_accessed=3 << 20, transcendentals=0),
        name="cross",
    )(info, queries, keys, values)


def merge(o_a, lse_a, o_b, lse_b):
    top = jnp.maximum(lse_a, lse_b)
    e_a = jnp.exp2(lse_a - top)
    e_b = jnp.exp2(lse_b - top)
    return ((o_a.astype(F32) * e_a + o_b.astype(F32) * e_b) / (e_a + e_b)).astype(BF)


def local(q, k, v, states, nb_shard, nb_row, wk, wv, wq):
    rows = q.shape[0]
    quarter = rows // 4
    y = lax.axis_index("y")
    z = lax.axis_index("z")
    x_lo = lax.axis_index("x_lo")
    core = lax.axis_index("core")
    late = lax.axis_index("x_hi") == 1
    db_index = lax.axis_index(DB)

    kv0, shard, row = lax.optimization_barrier((jnp.stack([k, v]), nb_shard, nb_row))

    place = 2 * lax.broadcasted_iota(jnp.int32, nb_shard.shape, 0) + lax.broadcasted_iota(
        jnp.int32, nb_shard.shape, 1
    )
    coded = place * states.shape[0] + row
    asked = shard == db_index
    none = nb_shard.size * states.shape[0]
    first = jnp.min(jnp.where(asked, coded, none)) & (states.shape[0] - 1)
    last = jnp.max(jnp.where(asked, coded, 0)) & (states.shape[0] - 1)
    pair = jnp.concatenate(
        [lax.dynamic_slice_in_dim(states, i, 1, 0) for i in (first, last)], axis=0
    )
    held_a = lax.all_gather(pair, "z", axis=0, tiled=True)

    kv1 = ring(kv0, "y", 1)
    kv2 = ring(kv0, "y", -1)
    qs = lax.ppermute(q, "x_hi", [(1, 0)])
    k3 = ring(kv1[0], "y", 1)
    v3 = ring(kv2[1], "y", -1)
    flags = jnp.stack([y < 0, y >= 1, y >= 3, y >= 2] + [~late] * 4).astype(jnp.int32)
    m, acc = attend_own(q, kv0)
    m, acc = attend_middle(flags, q, qs, m, acc, kv0, kv1, kv2)
    skip = 2 * wk.shape[0]
    cut = (wq.shape[0] - skip) // 2
    up, down = jnp.concatenate([wk, wv, wq[:cut]], axis=0), wq[cut:]
    up_x = ring(up, XX, -1)
    down_x = ring(down, XX, 1)
    o, o_sent, lse = attend_last(flags, q, qs, m, acc, k3, v3)
    lse, lse_sent = lse[0], lse[1]

    o_back = lax.ppermute(o_sent, "x_hi", [(0, 1)])
    lse_back = lax.ppermute(lse_sent, "x_hi", [(0, 1)])
    o_back, lse_back, up_x, down_x = lax.optimization_barrier((o_back, lse_back, up_x, down_x))
    ups = (up, swap(up, "core"), up_x, swap(up_x, "core"))
    downs = (down, swap(down, "core"), down_x, swap(down_x, "core"))
    wq4 = side_by_side(skip, ups, downs).reshape(8, -1, 4 * HD)

    lse_back = jnp.where(late, lse_back.reshape(rows, 1), LOW)
    self_out = merge(o, lse.reshape(rows, 1), o_back, lse_back)

    same = nb_shard.reshape(-1)[:, None] == nb_shard.reshape(-1)[None, :]
    n = nb_shard.size
    before = lax.broadcasted_iota(jnp.int32, (n, n), 1) < lax.broadcasted_iota(jnp.int32, (n, n), 0)
    rank = jnp.max((same & before).astype(jnp.int32), axis=1)
    shard = nb_shard.reshape(-1)
    slot = ((shard % 2) ^ core) * 16 + (shard // 4) * 2 + rank
    slot = jnp.where((shard // 2) % 2 == x_lo, slot, -1).reshape(4, n // 4)
    info = jnp.concatenate(
        [
            lax.dynamic_slice_in_dim(slot, 2 * x_lo + core, 1, 0),
            lax.dynamic_slice_in_dim(slot, 2 * (1 - x_lo) + core, 1, 0),
        ],
        axis=1,
    ).reshape(-1)

    mine = lax.all_to_all(self_out.reshape(4, quarter, HD), XC, 0, 0)
    f1 = ring(mine, "z", 1)
    b1 = ring(mine, "z", -1)
    f1, b1, held_a, wq4 = lax.optimization_barrier((f1, b1, held_a, wq4))
    held_b = swap(held_a, "core")
    f2 = ring(f1, "z", 1)
    b2 = ring(b1, "z", -1)
    f3 = ring(f2, "z", 1)
    b3 = ring(b2, "z", -1)
    keys, values = project(info, held_a, held_b, ups)
    f3, b3, keys, values = lax.optimization_barrier((f3, b3, keys, values))
    far_f = ring(f3[:2], "z", 1)
    far_b = ring(b3[2:], "z", -1)
    near = cross_queries(
        z, ((0, mine), (1, f1), (2, f2), (3, f3), (5, b3), (6, b2), (7, b1)), wq4
    )
    far_f, far_b, near = lax.optimization_barrier((far_f, far_b, near))
    far = jnp.concatenate([far_f, far_b], axis=0)
    queries = (near + cross_queries(z, ((4, far),), wq4)).astype(BF)

    other = swap(queries, "x_lo")
    o_a, lse_a = cross(0, info[: n // 4], queries, keys, values)
    got_a = swap(o_a[2:], "x_lo")
    other = jnp.concatenate([other[:, 2 * HD :], other[:, : 2 * HD]], axis=1)
    o_b, lse_b = cross(1, info[n // 4 :], other, keys, values)
    got_b = swap(o_b[2:], "x_lo")

    lse = jnp.stack([lse_a[:, :4], lse_b[:, :4]]).transpose(2, 0, 1, 3).reshape(4, 2, quarter, 1)
    lse_got = swap(lse[2:].reshape(2, 2, quarter), "x_lo")[..., None]
    both = jnp.stack(
        [
            merge(o_a[:2], lse[:2, 0], got_b, lse_got[:, 1]),
            merge(o_b[:2], lse[:2, 1], got_a, lse_got[:, 0]),
        ],
        axis=1,
    )
    kept, got = both[0], swap(both[1], "core")
    kept, got = (jnp.where(x_lo == 0, a, a[::-1]) for a in (kept, got))
    cross_out = jnp.where(
        core == 0, jnp.stack([kept, got], axis=1), jnp.stack([got, kept], axis=1)
    ).reshape(rows, HD)
    return (self_out, cross_out)


def solution(mesh):
    fine = Mesh(mesh.devices.reshape(2, 4, 8, 2, 2), AXES)
    return jax.shard_map(
        local,
        mesh=fine,
        in_specs=(
            P(CTX, DB),
            P(CTX, DB),
            P(CTX, DB),
            P(DB, None, None),
            P(CTX, None),
            P(CTX, None),
            P(None, DB),
            P(None, DB),
            P(None, DB),
        ),
        out_specs=(P(CTX, DB), P(CTX, DB)),
        check_vma=False,
    )
```

```python
import functools
import math

import jax
import jax.numpy as jnp
from jax import lax
from jax.experimental import pallas as pl
from jax.experimental.pallas import tpu as pltpu
from jax.sharding import Mesh
from jax.sharding import PartitionSpec as P

HD = 128
AXES = ("x_hi", "y", "z", "x_lo", "core")
CTX = ("x_hi", "y")
DB = ("z", "x_lo", "core")
XC = ("x_lo", "core")
XX = ("x_hi", "x_lo")
LOW = -1e30
EXP2_SCALE = math.log2(math.e) / math.sqrt(HD)
BF = jnp.bfloat16
F32 = jnp.float32


def ring(value, axis, step):
    n = lax.axis_size(axis)
    return lax.ppermute(value, axis, [(i, (i + step) % n) for i in range(n)])


def swap(value, axis):
    return lax.ppermute(value, axis, [(0, 1), (1, 0)])


def params(megabytes):
    return pltpu.CompilerParams(
        dimension_semantics=("arbitrary",), vmem_limit_bytes=megabytes << 20
    )


def dot_t(a, b):
    return lax.dot_general(a, b, (((1,), (1,)), ((), ())), preferred_element_type=F32)


SUB = 256


def load_block(kx, vx, key, value):
    kx[...] = key.T
    vx[:, :HD] = value
    vx[:, HD:] = jnp.ones_like(value)


def absorb(q_ref, kx, vx, m_ref, acc):
    def scores(i):
        return jnp.dot(q_ref[i * SUB : (i + 1) * SUB, :], kx[...], preferred_element_type=F32)

    n = q_ref.shape[0] // SUB
    s = scores(0)
    for i in range(n):
        ahead = scores(i + 1) if i + 1 < n else None
        r = slice(i * SUB, (i + 1) * SUB)
        before = m_ref[r]
        now = jnp.maximum(before, jnp.max(s, axis=1, keepdims=True))
        p = jnp.exp2((s - now[:, :1]) * EXP2_SCALE)
        factor = jnp.exp2((before - now) * EXP2_SCALE)
        m_ref[r] = now
        acc[r] = acc[r] * jnp.concatenate([factor, factor], axis=1) + jnp.dot(
            p.astype(BF), vx[...], preferred_element_type=F32
        )
        s = ahead


def own_kernel(q_ref, kv_ref, m_ref, acc, kx, vx):
    load_block(kx, vx, kv_ref[0], kv_ref[1])

    def scores(i):
        seen = (i + 1) * SUB
        s = jnp.dot(q_ref[i * SUB : seen, :], kx[:, :seen], preferred_element_type=F32)
        row = lax.broadcasted_iota(jnp.int32, s.shape, 0) + i * SUB
        return jnp.where(row >= lax.broadcasted_iota(jnp.int32, s.shape, 1), s, LOW)

    n = q_ref.shape[0] // SUB
    s = scores(0)
    for i in range(n):
        ahead = scores(i + 1) if i + 1 < n else None
        r = slice(i * SUB, (i + 1) * SUB)
        now = jnp.max(s, axis=1, keepdims=True)
        p = jnp.exp2((s - now) * EXP2_SCALE)
        m_ref[r] = jnp.broadcast_to(now, (SUB, HD))
        acc[r] = jnp.dot(p.astype(BF), vx[: (i + 1) * SUB, :], preferred_element_type=F32)
        s = ahead


def attend_own(q, kv):
    rows = q.shape[0]
    return pl.pallas_call(
        own_kernel,
        in_specs=[pl.BlockSpec(memory_space=pltpu.VMEM)] * 2,
        out_specs=[pl.BlockSpec(memory_space=pltpu.VMEM)] * 2,
        out_shape=[jax.ShapeDtypeStruct((rows, HD), F32), jax.ShapeDtypeStruct((rows, 2 * HD), F32)],
        scratch_shapes=[pltpu.VMEM((HD, rows), BF), pltpu.VMEM((rows, 2 * HD), BF)],
        compiler_params=pltpu.CompilerParams(vmem_limit_bytes=24 << 20),
        cost_estimate=pl.CostEstimate(flops=1 << 30, bytes_accessed=3 << 20, transcendentals=0),
        name="attend_own",
    )(q, kv)


def middle_kernel(flags, q_ref, qs_ref, m_in, acc_in, kv0, kv1, kv2, m_ref, acc, qx, kx, vx):
    which = pl.program_id(0)

    @pl.when(which == 0)
    def _():
        for b, kv in enumerate((kv0, kv1, kv2)):
            load_block(kx.at[b], vx.at[b], kv[0], kv[1])
        qx[...] = q_ref[...]
        m_ref[0] = m_in[...]
        acc[0] = acc_in[...]

    @pl.when(which == 1)
    def _():
        qx[...] = qs_ref[...]
        m_ref[0] = jnp.full(m_in.shape, LOW, F32)
        acc[0] = jnp.zeros(acc_in.shape, F32)

    @pl.loop(0, 3)
    def _(b):
        @pl.when(flags[4 * which + b] == 1)
        def _():
            absorb(qx, kx.at[b], vx.at[b], m_ref.at[0], acc.at[0])


def attend_middle(flags, q, qs, m, acc, kv0, kv1, kv2):
    rows = q.shape[0]
    whole2 = pl.BlockSpec((rows, HD), lambda t, f: (0, 0))
    whole3 = pl.BlockSpec((2, rows, HD), lambda t, f: (0, 0, 0))
    return pl.pallas_call(
        middle_kernel,
        grid_spec=pltpu.PrefetchScalarGridSpec(
            num_scalar_prefetch=1,
            grid=(2,),
            in_specs=[
                whole2,
                whole2,
                whole2,
                pl.BlockSpec((rows, 2 * HD), lambda t, f: (0, 0)),
                whole3,
                whole3,
                whole3,
            ],
            out_specs=[
                pl.BlockSpec((1, rows, HD), lambda t, f: (t, 0, 0)),
                pl.BlockSpec((1, rows, 2 * HD), lambda t, f: (t, 0, 0)),
            ],
            scratch_shapes=[
                pltpu.VMEM((rows, HD), BF),
                pltpu.VMEM((3, HD, rows), BF),
                pltpu.VMEM((3, rows, 2 * HD), BF),
            ],
        ),
        out_shape=[
            jax.ShapeDtypeStruct((2, rows, HD), F32),
            jax.ShapeDtypeStruct((2, rows, 2 * HD), F32),
        ],
        compiler_params=params(40),
        cost_estimate=pl.CostEstimate(flops=8 << 30, bytes_accessed=6 << 20, transcendentals=0),
        name="attend_middle",
    )(flags, q, qs, m, acc, kv0, kv1, kv2)


def last_kernel(flags, q_ref, qs_ref, m_in, acc_in, k3, v3, o_ref, os_ref, lse_ref, qx, kx, vx, m_ref, acc):
    which = pl.program_id(0)
    m_ref[...] = m_in[0]
    acc[...] = acc_in[0]

    @pl.when(which == 0)
    def _():
        load_block(kx, vx, k3[...], v3[...])
        qx[...] = q_ref[...]

    @pl.when(which == 1)
    def _():
        qx[...] = qs_ref[...]

    @pl.when(flags[4 * which + 3] == 1)
    def _():
        absorb(qx, kx, vx, m_ref, acc)

    total = acc[:, HD:]
    o = acc[:, :HD] / total
    lse = m_ref[...] * EXP2_SCALE + jnp.log2(total)
    for i in range(lse.shape[0] // SUB):
        lse_ref[0, i] = lse[i * SUB : (i + 1) * SUB].T[:1]

    @pl.when(which == 0)
    def _():
        o_ref[...] = o

    @pl.when(which == 1)
    def _():
        os_ref[...] = o.astype(BF)


def attend_last(flags, q, qs, m, acc, k3, v3):
    rows = q.shape[0]
    n = rows // SUB
    whole2 = pl.BlockSpec((rows, HD), lambda t, f: (0, 0))
    return pl.pallas_call(
        last_kernel,
        grid_spec=pltpu.PrefetchScalarGridSpec(
            num_scalar_prefetch=1,
            grid=(2,),
            in_specs=[
                whole2,
                whole2,
                pl.BlockSpec((1, rows, HD), lambda t, f: (t, 0, 0)),
                pl.BlockSpec((1, rows, 2 * HD), lambda t, f: (t, 0, 0)),
                whole2,
                whole2,
            ],
            out_specs=[whole2, whole2, pl.BlockSpec((1, n, 1, SUB), lambda t, f: (t, 0, 0, 0))],
            scratch_shapes=[
                pltpu.VMEM((rows, HD), BF),
                pltpu.VMEM((HD, rows), BF),
                pltpu.VMEM((rows, 2 * HD), BF),
                pltpu.VMEM((rows, HD), F32),
                pltpu.VMEM((rows, 2 * HD), F32),
            ],
        ),
        out_shape=[
            jax.ShapeDtypeStruct((rows, HD), F32),
            jax.ShapeDtypeStruct((rows, HD), BF),
            jax.ShapeDtypeStruct((2, n, 1, SUB), F32),
        ],
        compiler_params=params(40),
        cost_estimate=pl.CostEstimate(flops=3 << 30, bytes_accessed=6 << 20, transcendentals=0),
        name="attend_last",
    )(flags, q, qs, m, acc, k3, v3)


def pick_kernel(me, shard, row, states, out):
    first = last = jnp.int32(0)
    groups, per = shard.shape
    places = [(g, n) for g in range(groups) for n in range(per)]
    for g, n in places:
        last = jnp.where(shard[g, n] == me[0], row[g, n], last)
    for g, n in reversed(places):
        first = jnp.where(shard[g, n] == me[0], row[g, n], first)
    out[0] = states[first]
    out[1] = states[last]


def pick_pair(me, shard, row, states):
    return pl.pallas_call(
        pick_kernel,
        grid_spec=pltpu.PrefetchScalarGridSpec(
            num_scalar_prefetch=3,
            grid=(1,),
            in_specs=[pl.BlockSpec(states.shape, lambda t, a, b, c: (0, 0, 0))],
            out_specs=pl.BlockSpec((2,) + states.shape[1:], lambda t, a, b, c: (0, 0, 0)),
        ),
        out_shape=jax.ShapeDtypeStruct((2,) + states.shape[1:], states.dtype),
        compiler_params=params(24),
        cost_estimate=pl.CostEstimate(flops=1 << 20, bytes_accessed=4 << 20, transcendentals=0),
        name="pick_pair",
    )(me, shard, row, states)


def side_kernel(skip, u0, u1, u2, u3, d0, d1, d2, d3, out):
    cut = u0.shape[0] - skip
    for r, (u, d) in enumerate(((u0, d0), (u1, d1), (u2, d2), (u3, d3))):
        out[:cut, r * HD : (r + 1) * HD] = u[skip:]
        out[cut:, r * HD : (r + 1) * HD] = d[...]


def side_by_side(skip, ups, downs):
    depth = ups[0].shape[0] - skip + downs[0].shape[0]
    return pl.pallas_call(
        functools.partial(side_kernel, skip),
        in_specs=[pl.BlockSpec(memory_space=pltpu.VMEM)] * 8,
        out_specs=pl.BlockSpec(memory_space=pltpu.VMEM),
        out_shape=jax.ShapeDtypeStruct((depth, 4 * HD), BF),
        compiler_params=pltpu.CompilerParams(vmem_limit_bytes=24 << 20),
        cost_estimate=pl.CostEstimate(flops=1 << 20, bytes_accessed=10 << 20, transcendentals=0),
        name="side_by_side",
    )(*ups, *downs)


def cross_queries(z, parts, weights):
    total = 0.0
    for back, part in parts:
        a = jnp.concatenate([part[h] for h in range(part.shape[0])], axis=1)
        w = lax.dynamic_index_in_dim(weights, (z + 8 - back) % 8, 0, keepdims=False)
        total = total + jnp.dot(a, w, preferred_element_type=F32)
    return total


def project_kernel(info, a_ref, b_ref, w0, w1, w2, w3, k_ref, v_ref, w_ref):
    g = pl.program_id(0)
    slots = a_ref.shape[0]
    width = a_ref.shape[2]

    @pl.when(g == 0)
    def _():
        for r, piece in enumerate((w0, w1, w2, w3)):
            w_ref[:, r * HD : (r + 1) * HD] = piece[:width]
            w_ref[:, (4 + r) * HD : (5 + r) * HD] = piece[width:]

    def pick(n):
        slot = jnp.maximum(info[4 * g + n], 0)
        at = slot & (slots - 1)
        return jnp.where(slot < slots, a_ref[at], b_ref[at])

    states = jnp.concatenate([pick(n) for n in range(4)], axis=0)
    both = jnp.dot(states, w_ref[...], preferred_element_type=F32).astype(BF)
    half = both.shape[1] // 2
    for c in range(2):
        rows = slice(c * both.shape[0] // 2, (c + 1) * both.shape[0] // 2)
        k_ref[c] = both[rows, :half].T
        v_ref[c] = both[rows, half:]


def project(info, held_a, held_b, pieces):
    n, length, width = held_a.shape
    groups = info.shape[0] // 2
    half = 4 * HD
    whole = pl.BlockSpec((n, length, width), lambda g, s: (0, 0, 0))
    return pl.pallas_call(
        project_kernel,
        grid_spec=pltpu.PrefetchScalarGridSpec(
            num_scalar_prefetch=1,
            grid=(groups // 2,),
            in_specs=[whole, whole] + [pl.BlockSpec((2 * width, HD), lambda g, s: (0, 0))] * 4,
            out_specs=[
                pl.BlockSpec((2, half, 2 * length), lambda g, s: (g, 0, 0)),
                pl.BlockSpec((2, 2 * length, half), lambda g, s: (g, 0, 0)),
            ],
            scratch_shapes=[pltpu.VMEM((width, 2 * half), BF)],
        ),
        out_shape=[
            jax.ShapeDtypeStruct((groups, half, 2 * length), BF),
            jax.ShapeDtypeStruct((groups, 2 * length, half), BF),
        ],
        compiler_params=params(40),
        cost_estimate=pl.CostEstimate(flops=4 << 30, bytes_accessed=12 << 20, transcendentals=0),
        name="project",
    )(info, held_a, held_b, *pieces)


def cross_kernel(info, q_ref, k_ref, v_ref, o_ref, lse_ref):
    step = pl.program_id(0)
    per = k_ref.shape[0]
    group = lse_ref.shape[2]
    for c in range(per):
        rows = slice(c * group, (c + 1) * group)
        g = per * step + c
        q = q_ref[rows]
        first, second = info[2 * g] >= 0, info[2 * g + 1] >= 0
        column = lax.broadcasted_iota(jnp.int32, (1, k_ref.shape[2]), 1)
        bias = jnp.where(
            column < k_ref.shape[2] // 2, jnp.where(first, 0.0, LOW), jnp.where(second, 0.0, LOW)
        )
        some = first | second
        lane = lax.broadcasted_iota(jnp.int32, (group, HD), 1)
        stats = jnp.full((group, HD), LOW, F32)
        for r in range(4):
            cut = slice(r * HD, (r + 1) * HD)
            s = jnp.dot(q[:, cut], k_ref[c, cut, :], preferred_element_type=F32) + bias
            top = jnp.max(s, axis=1, keepdims=True)
            p = jnp.exp2((s - top) * EXP2_SCALE)
            total = jnp.sum(p, axis=1, keepdims=True)
            o = jnp.dot(p.astype(BF), v_ref[c, :, cut], preferred_element_type=F32) / total
            o_ref[r, rows] = o.astype(BF)
            stats = jnp.where((lane == r) & some, top * EXP2_SCALE + jnp.log2(total), stats)
        lse_ref[c] = stats.T[:8]


def cross(half, info, queries, keys, values):
    groups = keys.shape[0] // 2
    per = 2
    start = half * groups // per
    group = queries.shape[0] // groups
    width = queries.shape[1]
    return pl.pallas_call(
        cross_kernel,
        grid_spec=pltpu.PrefetchScalarGridSpec(
            num_scalar_prefetch=1,
            grid=(groups // per,),
            in_specs=[
                pl.BlockSpec((per * group, width), lambda g, s: (g, 0)),
                pl.BlockSpec((per,) + keys.shape[1:], lambda g, s: (start + g, 0, 0)),
                pl.BlockSpec((per,) + values.shape[1:], lambda g, s: (start + g, 0, 0)),
            ],
            out_specs=[
                pl.BlockSpec((4, per * group, HD), lambda g, s: (0, g, 0)),
                pl.BlockSpec((per, 8, group), lambda g, s: (g, 0, 0)),
            ],
        ),
        out_shape=[
            jax.ShapeDtypeStruct((4, groups * group, HD), BF),
            jax.ShapeDtypeStruct((groups, 8, group), F32),
        ],
        compiler_params=params(24),
        cost_estimate=pl.CostEstimate(flops=2 << 30, bytes_accessed=3 << 20, transcendentals=0),
        name="cross",
    )(info, queries, keys, values)


def merge(o_a, lse_a, o_b, lse_b):
    top = jnp.maximum(lse_a, lse_b)
    e_a = jnp.exp2(lse_a - top)
    e_b = jnp.exp2(lse_b - top)
    return ((o_a.astype(F32) * e_a + o_b.astype(F32) * e_b) / (e_a + e_b)).astype(BF)


def local(q, k, v, states, nb_shard, nb_row, wk, wv, wq):
    rows = q.shape[0]
    quarter = rows // 4
    y = lax.axis_index("y")
    z = lax.axis_index("z")
    x_lo = lax.axis_index("x_lo")
    core = lax.axis_index("core")
    late = lax.axis_index("x_hi") == 1
    db_index = lax.axis_index(DB)

    kv0, shard, row = lax.optimization_barrier((jnp.stack([k, v]), nb_shard, nb_row))

    pair = pick_pair(db_index.astype(jnp.int32)[None], shard, row, states)
    held_a = lax.all_gather(pair, "z", axis=0, tiled=True)

    kv1 = ring(kv0, "y", 1)
    kv2 = ring(kv0, "y", -1)
    qs = lax.ppermute(q, "x_hi", [(1, 0)])
    k3 = ring(kv1[0], "y", 1)
    v3 = ring(kv2[1], "y", -1)
    flags = jnp.stack([y < 0, y >= 1, y >= 3, y >= 2] + [~late] * 4).astype(jnp.int32)
    m, acc = attend_own(q, kv0)
    m, acc = attend_middle(flags, q, qs, m, acc, kv0, kv1, kv2)
    skip = 2 * wk.shape[0]
    cut = (wq.shape[0] - skip) // 2
    up, down = jnp.concatenate([wk, wv, wq[:cut]], axis=0), wq[cut:]
    up_x = ring(up, XX, -1)
    down_x = ring(down, XX, 1)
    o, o_sent, lse = attend_last(flags, q, qs, m, acc, k3, v3)
    lse, lse_sent = lse[0], lse[1]

    o_back = lax.ppermute(o_sent, "x_hi", [(0, 1)])
    lse_back = lax.ppermute(lse_sent, "x_hi", [(0, 1)])
    o_back, lse_back, up_x, down_x = lax.optimization_barrier((o_back, lse_back, up_x, down_x))
    ups = (up, swap(up, "core"), up_x, swap(up_x, "core"))
    downs = (down, swap(down, "core"), down_x, swap(down_x, "core"))
    wq4 = side_by_side(skip, ups, downs).reshape(8, -1, 4 * HD)

    lse_back = jnp.where(late, lse_back.reshape(rows, 1), LOW)
    self_out = merge(o, lse.reshape(rows, 1), o_back, lse_back)

    same = nb_shard.reshape(-1)[:, None] == nb_shard.reshape(-1)[None, :]
    n = nb_shard.size
    before = lax.broadcasted_iota(jnp.int32, (n, n), 1) < lax.broadcasted_iota(jnp.int32, (n, n), 0)
    rank = jnp.max((same & before).astype(jnp.int32), axis=1)
    shard = nb_shard.reshape(-1)
    slot = ((shard % 2) ^ core) * 16 + (shard // 4) * 2 + rank
    slot = jnp.where((shard // 2) % 2 == x_lo, slot, -1).reshape(4, n // 4)
    info = jnp.concatenate(
        [
            lax.dynamic_slice_in_dim(slot, 2 * x_lo + core, 1, 0),
            lax.dynamic_slice_in_dim(slot, 2 * (1 - x_lo) + core, 1, 0),
        ],
        axis=1,
    ).reshape(-1)

    mine = lax.all_to_all(self_out.reshape(4, quarter, HD), XC, 0, 0)
    f1 = ring(mine, "z", 1)
    b1 = ring(mine, "z", -1)
    f1, b1, held_a, wq4 = lax.optimization_barrier((f1, b1, held_a, wq4))
    held_b = swap(held_a, "core")
    f2 = ring(f1, "z", 1)
    b2 = ring(b1, "z", -1)
    f3 = ring(f2, "z", 1)
    b3 = ring(b2, "z", -1)
    keys, values = project(info, held_a, held_b, ups)
    f3, b3, keys, values = lax.optimization_barrier((f3, b3, keys, values))
    far_f = ring(f3[:2], "z", 1)
    far_b = ring(b3[2:], "z", -1)
    near = cross_queries(
        z, ((0, mine), (1, f1), (2, f2), (3, f3), (5, b3), (6, b2), (7, b1)), wq4
    )
    far_f, far_b, near = lax.optimization_barrier((far_f, far_b, near))
    far = jnp.concatenate([far_f, far_b], axis=0)
    queries = (near + cross_queries(z, ((4, far),), wq4)).astype(BF)

    other = swap(queries, "x_lo")
    o_a, lse_a = cross(0, info[: n // 4], queries, keys, values)
    got_a = swap(o_a[2:], "x_lo")
    other = jnp.concatenate([other[:, 2 * HD :], other[:, : 2 * HD]], axis=1)
    o_b, lse_b = cross(1, info[n // 4 :], other, keys, values)
    got_b = swap(o_b[2:], "x_lo")

    lse = jnp.stack([lse_a[:, :4], lse_b[:, :4]]).transpose(2, 0, 1, 3).reshape(4, 2, quarter, 1)
    lse_got = swap(lse[2:].reshape(2, 2, quarter), "x_lo")[..., None]
    both = jnp.stack(
        [
            merge(o_a[:2], lse[:2, 0], got_b, lse_got[:, 1]),
            merge(o_b[:2], lse[:2, 1], got_a, lse_got[:, 0]),
        ],
        axis=1,
    )
    kept, got = both[0], swap(both[1], "core")
    kept, got = (jnp.where(x_lo == 0, a, a[::-1]) for a in (kept, got))
    cross_out = jnp.where(
        core == 0, jnp.stack([kept, got], axis=1), jnp.stack([got, kept], axis=1)
    ).reshape(rows, HD)
    return (self_out, cross_out)


def solution(mesh):
    fine = Mesh(mesh.devices.reshape(2, 4, 8, 2, 2), AXES)
    return jax.shard_map(
        local,
        mesh=fine,
        in_specs=(
            P(CTX, DB),
            P(CTX, DB),
            P(CTX, DB),
            P(DB, None, None),
            P(CTX, None),
            P(CTX, None),
            P(None, DB),
            P(None, DB),
            P(None, DB),
        ),
        out_specs=(P(CTX, DB), P(CTX, DB)),
        check_vma=False,
    )
```

```python
import functools
import math

import jax
import jax.numpy as jnp
from jax import lax
from jax.experimental import pallas as pl
from jax.experimental.pallas import tpu as pltpu
from jax.sharding import Mesh
from jax.sharding import PartitionSpec as P

HD = 128
AXES = ("x_hi", "y", "z", "x_lo", "core")
CTX = ("x_hi", "y")
DB = ("z", "x_lo", "core")
XC = ("x_lo", "core")
XX = ("x_hi", "x_lo")
LOW = -1e30
EXP2_SCALE = math.log2(math.e) / math.sqrt(HD)
BF = jnp.bfloat16
F32 = jnp.float32


def ring(value, axis, step):
    n = lax.axis_size(axis)
    return lax.ppermute(value, axis, [(i, (i + step) % n) for i in range(n)])


def swap(value, axis):
    return lax.ppermute(value, axis, [(0, 1), (1, 0)])


def params(megabytes):
    return pltpu.CompilerParams(
        dimension_semantics=("arbitrary",), vmem_limit_bytes=megabytes << 20
    )


def dot_t(a, b):
    return lax.dot_general(a, b, (((1,), (1,)), ((), ())), preferred_element_type=F32)


SUB = 256


def load_block(kx, vx, key, value):
    kx[...] = key.T
    vx[:, :HD] = value
    vx[:, HD:] = jnp.ones_like(value)


def absorb(q_ref, kx, vx, m_ref, acc):
    def scores(i):
        return jnp.dot(q_ref[i * SUB : (i + 1) * SUB, :], kx[...], preferred_element_type=F32)

    n = q_ref.shape[0] // SUB
    s = scores(0)
    for i in range(n):
        ahead = scores(i + 1) if i + 1 < n else None
        r = slice(i * SUB, (i + 1) * SUB)
        before = m_ref[r]
        now = jnp.maximum(before, jnp.max(s, axis=1, keepdims=True))
        p = jnp.exp2((s - now[:, :1]) * EXP2_SCALE)
        factor = jnp.exp2((before - now) * EXP2_SCALE)
        m_ref[r] = now
        acc[r] = acc[r] * jnp.concatenate([factor, factor], axis=1) + jnp.dot(
            p.astype(BF), vx[...], preferred_element_type=F32
        )
        s = ahead


def own_kernel(q_ref, kv_ref, m_ref, acc, kx, vx):
    load_block(kx, vx, kv_ref[0], kv_ref[1])

    def scores(i):
        seen = (i + 1) * SUB
        s = jnp.dot(q_ref[i * SUB : seen, :], kx[:, :seen], preferred_element_type=F32)
        row = lax.broadcasted_iota(jnp.int32, s.shape, 0) + i * SUB
        return jnp.where(row >= lax.broadcasted_iota(jnp.int32, s.shape, 1), s, LOW)

    n = q_ref.shape[0] // SUB
    s = scores(0)
    for i in range(n):
        ahead = scores(i + 1) if i + 1 < n else None
        r = slice(i * SUB, (i + 1) * SUB)
        now = jnp.max(s, axis=1, keepdims=True)
        p = jnp.exp2((s - now) * EXP2_SCALE)
        m_ref[r] = jnp.broadcast_to(now, (SUB, HD))
        acc[r] = jnp.dot(p.astype(BF), vx[: (i + 1) * SUB, :], preferred_element_type=F32)
        s = ahead


def attend_own(q, kv):
    rows = q.shape[0]
    return pl.pallas_call(
        own_kernel,
        in_specs=[pl.BlockSpec(memory_space=pltpu.VMEM)] * 2,
        out_specs=[pl.BlockSpec(memory_space=pltpu.VMEM)] * 2,
        out_shape=[jax.ShapeDtypeStruct((rows, HD), F32), jax.ShapeDtypeStruct((rows, 2 * HD), F32)],
        scratch_shapes=[pltpu.VMEM((HD, rows), BF), pltpu.VMEM((rows, 2 * HD), BF)],
        compiler_params=pltpu.CompilerParams(vmem_limit_bytes=24 << 20),
        cost_estimate=pl.CostEstimate(flops=1 << 30, bytes_accessed=3 << 20, transcendentals=0),
        name="attend_own",
    )(q, kv)


def middle_kernel(flags, q_ref, qs_ref, m_in, acc_in, kv0, kv1, kv2, m_ref, acc, qx, kx, vx):
    which = pl.program_id(0)

    @pl.when(which == 0)
    def _():
        for b, kv in enumerate((kv0, kv1, kv2)):
            load_block(kx.at[b], vx.at[b], kv[0], kv[1])
        qx[...] = q_ref[...]
        m_ref[0] = m_in[...]
        acc[0] = acc_in[...]

    @pl.when(which == 1)
    def _():
        qx[...] = qs_ref[...]
        m_ref[0] = jnp.full(m_in.shape, LOW, F32)
        acc[0] = jnp.zeros(acc_in.shape, F32)

    @pl.loop(0, 3)
    def _(b):
        @pl.when(flags[4 * which + b] == 1)
        def _():
            absorb(qx, kx.at[b], vx.at[b], m_ref.at[0], acc.at[0])


def attend_middle(flags, q, qs, m, acc, kv0, kv1, kv2):
    rows = q.shape[0]
    whole2 = pl.BlockSpec((rows, HD), lambda t, f: (0, 0))
    whole3 = pl.BlockSpec((2, rows, HD), lambda t, f: (0, 0, 0))
    return pl.pallas_call(
        middle_kernel,
        grid_spec=pltpu.PrefetchScalarGridSpec(
            num_scalar_prefetch=1,
            grid=(2,),
            in_specs=[
                whole2,
                whole2,
                whole2,
                pl.BlockSpec((rows, 2 * HD), lambda t, f: (0, 0)),
                whole3,
                whole3,
                whole3,
            ],
            out_specs=[
                pl.BlockSpec((1, rows, HD), lambda t, f: (t, 0, 0)),
                pl.BlockSpec((1, rows, 2 * HD), lambda t, f: (t, 0, 0)),
            ],
            scratch_shapes=[
                pltpu.VMEM((rows, HD), BF),
                pltpu.VMEM((3, HD, rows), BF),
                pltpu.VMEM((3, rows, 2 * HD), BF),
            ],
        ),
        out_shape=[
            jax.ShapeDtypeStruct((2, rows, HD), F32),
            jax.ShapeDtypeStruct((2, rows, 2 * HD), F32),
        ],
        compiler_params=params(40),
        cost_estimate=pl.CostEstimate(flops=8 << 30, bytes_accessed=6 << 20, transcendentals=0),
        name="attend_middle",
    )(flags, q, qs, m, acc, kv0, kv1, kv2)


def last_kernel(flags, q_ref, qs_ref, m_in, acc_in, k3, v3, o_ref, os_ref, lse_ref, qx, kx, vx, m_ref, acc):
    which = pl.program_id(0)
    m_ref[...] = m_in[0]
    acc[...] = acc_in[0]

    @pl.when(which == 0)
    def _():
        load_block(kx, vx, k3[...], v3[...])
        qx[...] = q_ref[...]

    @pl.when(which == 1)
    def _():
        qx[...] = qs_ref[...]

    @pl.when(flags[4 * which + 3] == 1)
    def _():
        absorb(qx, kx, vx, m_ref, acc)

    total = acc[:, HD:]
    o = acc[:, :HD] / total
    lse = m_ref[...] * EXP2_SCALE + jnp.log2(total)
    for i in range(lse.shape[0] // SUB):
        lse_ref[0, i] = lse[i * SUB : (i + 1) * SUB].T[:1]

    @pl.when(which == 0)
    def _():
        o_ref[...] = o

    @pl.when(which == 1)
    def _():
        os_ref[...] = o.astype(BF)


def attend_last(flags, q, qs, m, acc, k3, v3):
    rows = q.shape[0]
    n = rows // SUB
    whole2 = pl.BlockSpec((rows, HD), lambda t, f: (0, 0))
    return pl.pallas_call(
        last_kernel,
        grid_spec=pltpu.PrefetchScalarGridSpec(
            num_scalar_prefetch=1,
            grid=(2,),
            in_specs=[
                whole2,
                whole2,
                pl.BlockSpec((1, rows, HD), lambda t, f: (t, 0, 0)),
                pl.BlockSpec((1, rows, 2 * HD), lambda t, f: (t, 0, 0)),
                whole2,
                whole2,
            ],
            out_specs=[whole2, whole2, pl.BlockSpec((1, n, 1, SUB), lambda t, f: (t, 0, 0, 0))],
            scratch_shapes=[
                pltpu.VMEM((rows, HD), BF),
                pltpu.VMEM((HD, rows), BF),
                pltpu.VMEM((rows, 2 * HD), BF),
                pltpu.VMEM((rows, HD), F32),
                pltpu.VMEM((rows, 2 * HD), F32),
            ],
        ),
        out_shape=[
            jax.ShapeDtypeStruct((rows, HD), F32),
            jax.ShapeDtypeStruct((rows, HD), BF),
            jax.ShapeDtypeStruct((2, n, 1, SUB), F32),
        ],
        compiler_params=params(40),
        cost_estimate=pl.CostEstimate(flops=3 << 30, bytes_accessed=6 << 20, transcendentals=0),
        name="attend_last",
    )(flags, q, qs, m, acc, k3, v3)


def side_kernel(skip, u0, u1, u2, u3, d0, d1, d2, d3, out):
    cut = u0.shape[0] - skip
    for r, (u, d) in enumerate(((u0, d0), (u1, d1), (u2, d2), (u3, d3))):
        out[:cut, r * HD : (r + 1) * HD] = u[skip:]
        out[cut:, r * HD : (r + 1) * HD] = d[...]


def side_by_side(skip, ups, downs):
    depth = ups[0].shape[0] - skip + downs[0].shape[0]
    return pl.pallas_call(
        functools.partial(side_kernel, skip),
        in_specs=[pl.BlockSpec(memory_space=pltpu.VMEM)] * 8,
        out_specs=pl.BlockSpec(memory_space=pltpu.VMEM),
        out_shape=jax.ShapeDtypeStruct((depth, 4 * HD), BF),
        compiler_params=pltpu.CompilerParams(vmem_limit_bytes=24 << 20),
        cost_estimate=pl.CostEstimate(flops=1 << 20, bytes_accessed=10 << 20, transcendentals=0),
        name="side_by_side",
    )(*ups, *downs)


def cross_queries(z, parts, weights):
    total = 0.0
    for back, part in parts:
        a = jnp.concatenate([part[h] for h in range(part.shape[0])], axis=1)
        w = lax.dynamic_index_in_dim(weights, (z + 8 - back) % 8, 0, keepdims=False)
        total = total + jnp.dot(a, w, preferred_element_type=F32)
    return total


def project_kernel(info, a_ref, b_ref, w0, w1, w2, w3, k_ref, v_ref, w_ref):
    g = pl.program_id(0)
    slots = a_ref.shape[0]
    width = a_ref.shape[2]

    @pl.when(g == 0)
    def _():
        for r, piece in enumerate((w0, w1, w2, w3)):
            w_ref[:, r * HD : (r + 1) * HD] = piece[:width]
            w_ref[:, (4 + r) * HD : (5 + r) * HD] = piece[width:]

    def pick(n):
        slot = jnp.maximum(info[4 * g + n], 0)
        at = slot & (slots - 1)
        return jnp.where(slot < slots, a_ref[at], b_ref[at])

    states = jnp.concatenate([pick(n) for n in range(4)], axis=0)
    both = jnp.dot(states, w_ref[...], preferred_element_type=F32).astype(BF)
    half = both.shape[1] // 2
    for c in range(2):
        rows = slice(c * both.shape[0] // 2, (c + 1) * both.shape[0] // 2)
        k_ref[c] = both[rows, :half].T
        v_ref[c] = both[rows, half:]


def project(info, held_a, held_b, pieces):
    n, length, width = held_a.shape
    groups = info.shape[0] // 2
    half = 4 * HD
    whole = pl.BlockSpec((n, length, width), lambda g, s: (0, 0, 0))
    return pl.pallas_call(
        project_kernel,
        grid_spec=pltpu.PrefetchScalarGridSpec(
            num_scalar_prefetch=1,
            grid=(groups // 2,),
            in_specs=[whole, whole] + [pl.BlockSpec((2 * width, HD), lambda g, s: (0, 0))] * 4,
            out_specs=[
                pl.BlockSpec((2, half, 2 * length), lambda g, s: (g, 0, 0)),
                pl.BlockSpec((2, 2 * length, half), lambda g, s: (g, 0, 0)),
            ],
            scratch_shapes=[pltpu.VMEM((width, 2 * half), BF)],
        ),
        out_shape=[
            jax.ShapeDtypeStruct((groups, half, 2 * length), BF),
            jax.ShapeDtypeStruct((groups, 2 * length, half), BF),
        ],
        compiler_params=params(40),
        cost_estimate=pl.CostEstimate(flops=4 << 30, bytes_accessed=12 << 20, transcendentals=0),
        name="project",
    )(info, held_a, held_b, *pieces)


def cross_kernel(info, q_ref, k_ref, v_ref, o_ref, lse_ref):
    step = pl.program_id(0)
    per = k_ref.shape[0]
    group = lse_ref.shape[2]
    for c in range(per):
        rows = slice(c * group, (c + 1) * group)
        g = per * step + c
        q = q_ref[rows]
        first, second = info[2 * g] >= 0, info[2 * g + 1] >= 0
        column = lax.broadcasted_iota(jnp.int32, (1, k_ref.shape[2]), 1)
        bias = jnp.where(
            column < k_ref.shape[2] // 2, jnp.where(first, 0.0, LOW), jnp.where(second, 0.0, LOW)
        )
        some = first | second
        lane = lax.broadcasted_iota(jnp.int32, (group, HD), 1)
        stats = jnp.full((group, HD), LOW, F32)
        for r in range(4):
            cut = slice(r * HD, (r + 1) * HD)
            s = jnp.dot(q[:, cut], k_ref[c, cut, :], preferred_element_type=F32) + bias
            top = jnp.max(s, axis=1, keepdims=True)
            p = jnp.exp2((s - top) * EXP2_SCALE)
            total = jnp.sum(p, axis=1, keepdims=True)
            o = jnp.dot(p.astype(BF), v_ref[c, :, cut], preferred_element_type=F32) / total
            o_ref[r, rows] = o.astype(BF)
            stats = jnp.where((lane == r) & some, top * EXP2_SCALE + jnp.log2(total), stats)
        lse_ref[c] = stats.T[:8]


def cross(half, info, queries, keys, values):
    groups = keys.shape[0] // 2
    per = 2
    start = half * groups // per
    group = queries.shape[0] // groups
    width = queries.shape[1]
    return pl.pallas_call(
        cross_kernel,
        grid_spec=pltpu.PrefetchScalarGridSpec(
            num_scalar_prefetch=1,
            grid=(groups // per,),
            in_specs=[
                pl.BlockSpec((per * group, width), lambda g, s: (g, 0)),
                pl.BlockSpec((per,) + keys.shape[1:], lambda g, s: (start + g, 0, 0)),
                pl.BlockSpec((per,) + values.shape[1:], lambda g, s: (start + g, 0, 0)),
            ],
            out_specs=[
                pl.BlockSpec((4, per * group, HD), lambda g, s: (0, g, 0)),
                pl.BlockSpec((per, 8, group), lambda g, s: (g, 0, 0)),
            ],
        ),
        out_shape=[
            jax.ShapeDtypeStruct((4, groups * group, HD), BF),
            jax.ShapeDtypeStruct((groups, 8, group), F32),
        ],
        compiler_params=params(24),
        cost_estimate=pl.CostEstimate(flops=2 << 30, bytes_accessed=3 << 20, transcendentals=0),
        name="cross",
    )(info, queries, keys, values)


def merge(o_a, lse_a, o_b, lse_b):
    top = jnp.maximum(lse_a, lse_b)
    e_a = jnp.exp2(lse_a - top)
    e_b = jnp.exp2(lse_b - top)
    return ((o_a.astype(F32) * e_a + o_b.astype(F32) * e_b) / (e_a + e_b)).astype(BF)


def local(q, k, v, states, nb_shard, nb_row, wk, wv, wq):
    rows = q.shape[0]
    quarter = rows // 4
    y = lax.axis_index("y")
    z = lax.axis_index("z")
    x_lo = lax.axis_index("x_lo")
    core = lax.axis_index("core")
    late = lax.axis_index("x_hi") == 1
    db_index = lax.axis_index(DB)

    kv0 = jnp.stack([k, v])
    qs = lax.ppermute(q, "x_hi", [(1, 0)])
    kv1 = ring(kv0, "y", 1)
    kv1, shard, row = lax.optimization_barrier((kv1, nb_shard, nb_row))

    place = 2 * lax.broadcasted_iota(jnp.int32, nb_shard.shape, 0) + lax.broadcasted_iota(
        jnp.int32, nb_shard.shape, 1
    )
    coded = place * states.shape[0] + row
    asked = shard == db_index
    none = nb_shard.size * states.shape[0]
    first = jnp.min(jnp.where(asked, coded, none)) & (states.shape[0] - 1)
    last = jnp.max(jnp.where(asked, coded, 0)) & (states.shape[0] - 1)
    pair = jnp.concatenate(
        [lax.dynamic_slice_in_dim(states, i, 1, 0) for i in (first, last)], axis=0
    )
    held_a = lax.all_gather(pair, "z", axis=0, tiled=True)

    kv2 = ring(kv0, "y", -1)
    k3 = ring(kv1[0], "y", 1)
    v3 = ring(kv2[1], "y", -1)
    flags = jnp.stack([y < 0, y >= 1, y >= 3, y >= 2] + [~late] * 4).astype(jnp.int32)
    m, acc = attend_own(q, kv0)
    m, acc = attend_middle(flags, q, qs, m, acc, kv0, kv1, kv2)
    skip = 2 * wk.shape[0]
    cut = (wq.shape[0] - skip) // 2
    up, down = jnp.concatenate([wk, wv, wq[:cut]], axis=0), wq[cut:]
    up_x = ring(up, XX, -1)
    down_x = ring(down, XX, 1)
    o, o_sent, lse = attend_last(flags, q, qs, m, acc, k3, v3)
    lse, lse_sent = lse[0], lse[1]

    o_back = lax.ppermute(o_sent, "x_hi", [(0, 1)])
    lse_back = lax.ppermute(lse_sent, "x_hi", [(0, 1)])
    o_back, lse_back, up_x, down_x = lax.optimization_barrier((o_back, lse_back, up_x, down_x))
    ups = (up, swap(up, "core"), up_x, swap(up_x, "core"))
    downs = (down, swap(down, "core"), down_x, swap(down_x, "core"))
    wq4 = side_by_side(skip, ups, downs).reshape(8, -1, 4 * HD)

    lse_back = jnp.where(late, lse_back.reshape(rows, 1), LOW)
    self_out = merge(o, lse.reshape(rows, 1), o_back, lse_back)

    same = nb_shard.reshape(-1)[:, None] == nb_shard.reshape(-1)[None, :]
    n = nb_shard.size
    before = lax.broadcasted_iota(jnp.int32, (n, n), 1) < lax.broadcasted_iota(jnp.int32, (n, n), 0)
    rank = jnp.max((same & before).astype(jnp.int32), axis=1)
    shard = nb_shard.reshape(-1)
    slot = ((shard % 2) ^ core) * 16 + (shard // 4) * 2 + rank
    slot = jnp.where((shard // 2) % 2 == x_lo, slot, -1).reshape(4, n // 4)
    info = jnp.concatenate(
        [
            lax.dynamic_slice_in_dim(slot, 2 * x_lo + core, 1, 0),
            lax.dynamic_slice_in_dim(slot, 2 * (1 - x_lo) + core, 1, 0),
        ],
        axis=1,
    ).reshape(-1)

    mine = lax.all_to_all(self_out.reshape(4, quarter, HD), XC, 0, 0)
    f1 = ring(mine, "z", 1)
    b1 = ring(mine, "z", -1)
    f1, b1, wq4 = lax.optimization_barrier((f1, b1, wq4))
    f2 = ring(f1, "z", 1)
    b2 = ring(b1, "z", -1)
    f2, b2, held_a = lax.optimization_barrier((f2, b2, held_a))
    held_b = swap(held_a, "core")
    f3 = ring(f2, "z", 1)
    b3 = ring(b2, "z", -1)
    keys, values = project(info, held_a, held_b, ups)
    f3, b3, keys, values = lax.optimization_barrier((f3, b3, keys, values))
    far_f = ring(f3[:2], "z", 1)
    far_b = ring(b3[2:], "z", -1)
    near = cross_queries(
        z, ((0, mine), (1, f1), (2, f2), (3, f3), (5, b3), (6, b2), (7, b1)), wq4
    )
    far_f, far_b, near = lax.optimization_barrier((far_f, far_b, near))
    far = jnp.concatenate([far_f, far_b], axis=0)
    queries = (near + cross_queries(z, ((4, far),), wq4)).astype(BF)

    other = swap(queries, "x_lo")
    o_a, lse_a = cross(0, info[: n // 4], queries, keys, values)
    got_a = swap(o_a[2:], "x_lo")
    other = jnp.concatenate([other[:, 2 * HD :], other[:, : 2 * HD]], axis=1)
    o_b, lse_b = cross(1, info[n // 4 :], other, keys, values)
    got_b = swap(o_b[2:], "x_lo")

    lse = jnp.stack([lse_a[:, :4], lse_b[:, :4]]).transpose(2, 0, 1, 3).reshape(4, 2, quarter, 1)
    lse_got = swap(lse[2:].reshape(2, 2, quarter), "x_lo")[..., None]
    both = jnp.stack(
        [
            merge(o_a[:2], lse[:2, 0], got_b, lse_got[:, 1]),
            merge(o_b[:2], lse[:2, 1], got_a, lse_got[:, 0]),
        ],
        axis=1,
    )
    kept, got = both[0], swap(both[1], "core")
    kept, got = (jnp.where(x_lo == 0, a, a[::-1]) for a in (kept, got))
    cross_out = jnp.where(
        core == 0, jnp.stack([kept, got], axis=1), jnp.stack([got, kept], axis=1)
    ).reshape(rows, HD)
    return (self_out, cross_out)


def solution(mesh):
    fine = Mesh(mesh.devices.reshape(2, 4, 8, 2, 2), AXES)
    return jax.shard_map(
        local,
        mesh=fine,
        in_specs=(
            P(CTX, DB),
            P(CTX, DB),
            P(CTX, DB),
            P(DB, None, None),
            P(CTX, None),
            P(CTX, None),
            P(None, DB),
            P(None, DB),
            P(None, DB),
        ),
        out_specs=(P(CTX, DB), P(CTX, DB)),
        check_vma=False,
    )
```
